256 devices in a mesh: row: 2 (over y_hi), col: 4 (over x), frame: 32 (over z, y_lo, core).
Axes of the slice: x: 4, y: 4 (y_hi: 2, y_lo: 2; y = y_hi * 2 + y_lo), z: 8, core: 2. Of those that a mesh axis runs over, the one named last changes fastest.
Arguments:
- video: float32 [128, 576, 1024], P('frame', 'row', 'col'), may hold values from -60 to 60
- multiplier: float32 [128, 576, 1024], P('frame', 'row', 'col'), may hold values from -3 to 3
- foreground: float32 [128, 576, 1024], P('frame', 'row', 'col'), may hold values from -6 to 6
- basis: float32 [16, 576, 1024], P(None, 'row', 'col'), may hold values from -40 to 40
- coefficients: float32 [128, 16], P('frame'), may hold values from -10 to 10
Outputs:
- new_foreground: float32 [128, 576, 1024], P('frame', 'row', 'col')
- new_coefficients: float32 [128, 16], P('frame')
- new_basis: float32 [16, 576, 1024], P(None, ('row', 'frame'), 'col')
The draws below stay inside these ranges and needn't reach their ends.
All inputs are finite; a program needn't handle non-finite values.
Results may differ from the reference program's by a relative error of at most 0.0003.
Values sent between devices are 32-bit elements; how exact they have to be, the bound alone decides.
No kernel may reach another device: no remote copies, remote signals or barrier semaphores. Data moves between devices by JAX's collectives and lax.ppermute only.
A program may use at most 128 MiB of HBM per device.

```python
import jax
import jax.numpy as jnp
from jax import lax

RANK = 16
PASSES = 3
FRAMES = 128
HEIGHT = 576
WIDTH = 1024


def factor_parts(key):
    folded = jax.random.fold_in(key, 101)
    streams = jax.random.split(folded, 6)
    rank_scale = jnp.exp(jax.random.uniform(streams[0], (RANK,), jnp.float32, -1.15, 1.15))
    rise_rows = 3.0 ** (jnp.arange(HEIGHT, dtype=jnp.float32) / HEIGHT - 0.5)
    rise_cols = 3.0 ** (jnp.arange(WIDTH, dtype=jnp.float32) / WIDTH - 0.5)
    pixel_scale = jnp.exp(jax.random.uniform(streams[1], (HEIGHT, WIDTH), jnp.float32, -1.15, 1.15)) * rise_rows[:, None] * rise_cols[None, :]
    shapes = jax.random.normal(streams[2], (RANK, HEIGHT, WIDTH), jnp.float32)
    true_basis = 0.5 * shapes * rank_scale[:, None, None] * pixel_scale[None, :, :]
    frame_scale = jnp.exp(jax.random.uniform(streams[4], (FRAMES,), jnp.float32, -1.15, 1.15)) * 3.0 ** (jnp.arange(FRAMES, dtype=jnp.float32) / FRAMES - 0.5)
    weights = jax.random.normal(streams[5], (FRAMES, RANK), jnp.float32)
    true_coeff = 0.25 * weights * frame_scale[:, None]
    return (true_basis, true_coeff)


def draw_video(key, part):
    true_basis, true_coeff = factor_parts(key)
    streams = jax.random.split(jax.random.fold_in(key, 202), 3)
    low_rank = jnp.einsum('fr,rhw->fhw', true_coeff, true_basis)
    spikes = 2.0 * jax.random.normal(streams[1], (FRAMES, HEIGHT, WIDTH), jnp.float32) * jax.random.bernoulli(streams[2], 0.1, (FRAMES, HEIGHT, WIDTH)).astype(jnp.float32)
    jitter = 0.3 * jax.random.normal(streams[0], (FRAMES, HEIGHT, WIDTH), jnp.float32)
    return jnp.clip(low_rank + jitter + spikes, -60.0, 60.0)


def draw_basis(key, part):
    true_basis, true_coeff = factor_parts(key)
    jitter = jax.random.normal(jax.random.fold_in(key, 303), (RANK, HEIGHT, WIDTH), jnp.float32)
    return jnp.clip(true_basis * (1.0 + 0.2 * jitter), -40.0, 40.0)


def draw_coefficients(key, part):
    true_basis, true_coeff = factor_parts(key)
    jitter = jax.random.normal(jax.random.fold_in(key, 404), (FRAMES, RANK), jnp.float32)
    return jnp.clip(true_coeff + 0.1 * jitter, -10.0, 10.0)


def block_scale(key, dims, pieces, least, top_value):
    level, own = 1.0, jax.random.fold_in(key, 6)
    for position, parts in pieces:
        draws = jnp.exp(jax.random.uniform(jax.random.fold_in(own, position), (parts,), jnp.float32, least / len(pieces), top_value / len(pieces)))
        level = level * jnp.repeat(draws, dims[position] // parts).reshape([-1 if axis == position else 1 for axis in range(len(dims))])
    return level


def centred(key, shape, scale, bound, cuts=(), kind=jnp.bfloat16):
    result = jax.random.normal(key, shape, jnp.float32) * scale
    if len(cuts) > 0:
        result = block_scale(key, shape, cuts, -0.22, 0.18) * result
    return jnp.clip(result, min=-bound, max=bound).astype(kind)


def setup_inputs(seed: int = 0) -> dict:
    arg_keys = jax.random.split(jax.random.key(seed), 6)
    video = draw_video(jax.random.fold_in(arg_keys[5], 71), 0)
    multiplier = centred(arg_keys[1], (FRAMES, HEIGHT, WIDTH), 0.5, 3.0, ((0, 32), (1, 2), (2, 4)), jnp.float32)
    foreground = centred(arg_keys[2], (FRAMES, HEIGHT, WIDTH), 1.0, 6.0, ((0, 32), (1, 2), (2, 4)), jnp.float32)
    basis = draw_basis(jax.random.fold_in(arg_keys[5], 71), 0)
    coefficients = draw_coefficients(jax.random.fold_in(arg_keys[5], 71), 0)
    return dict(video=video, multiplier=multiplier, foreground=foreground, basis=basis, coefficients=coefficients)


relax_rate = 0.8
smooth_weight = 0.5
smooth_floor = 0.25
shrink_level = 0.4
dual_scale = 0.8
ridge_share = 0.1

def forward_cells(padded, direction, shape):
    starts = [0, 0, 0]
    starts[direction] = 1
    limits = [starts[axis_dim] + shape[axis_dim] for axis_dim in range(3)]
    return lax.slice(padded, starts, limits)

def descend(padded, source, anchor, extent):
    shape = tuple((int(length) - 1 for length in padded.shape))
    here_cells = padded[:-1, :-1, :-1]
    slopes = []
    for direction in range(3):
        ahead_cells = forward_cells(padded, direction, shape)
        places = anchor[direction] + jnp.arange(shape[direction], dtype=jnp.int32)
        inside = (places >= 0) & (places < extent[direction] - 1)
        layout = [1, 1, 1]
        layout[direction] = shape[direction]
        inside = inside.reshape(layout)
        slopes.append(jnp.where(inside, ahead_cells - here_cells, jnp.zeros_like(here_cells)))
    weight = lax.rsqrt(smooth_floor + slopes[0] * slopes[0] + slopes[1] * slopes[1] + slopes[2] * slopes[2])
    fluxes = [slope_part * weight for slope_part in slopes]
    spread = fluxes[0][1:, 1:, 1:] - fluxes[0][:-1, 1:, 1:] + (fluxes[1][1:, 1:, 1:] - fluxes[1][1:, :-1, 1:]) + (fluxes[2][1:, 1:, 1:] - fluxes[2][1:, 1:, :-1])
    center = padded[1:-1, 1:-1, 1:-1]
    return center + relax_rate * (source - center + smooth_weight * spread)

def solve_definite(matrix, right_side):
    factor_lower = jnp.linalg.cholesky(matrix)
    half_solved = lax.linalg.triangular_solve(factor_lower, right_side, left_side=True, lower=True)
    return lax.linalg.triangular_solve(factor_lower, half_solved, left_side=True, lower=True, transpose_a=True)

def reference(video, multiplier, foreground, basis, coefficients):
    highest = lax.Precision.HIGHEST
    flat_basis = basis.reshape(RANK, HEIGHT * WIDTH)
    background = jnp.dot(coefficients, flat_basis, precision=highest).reshape(FRAMES, HEIGHT, WIDTH)
    target = video - background + dual_scale * multiplier
    current = foreground
    for sweep in range(PASSES):
        padded = jnp.pad(current, 1)
        current = descend(padded, target, (-1, -1, -1), (FRAMES, HEIGHT, WIDTH))
    shrunk = current - jnp.clip(current, -shrink_level, shrink_level)
    residual_target = video + dual_scale * multiplier - shrunk
    flat_target = residual_target.reshape(FRAMES, HEIGHT * WIDTH)
    gram_sum = jnp.dot(flat_basis, flat_basis.T, precision=highest)
    cross_sum = jnp.dot(flat_basis, flat_target.T, precision=highest)
    identity_matrix = jnp.eye(RANK, dtype=gram_sum.dtype)
    pixel_ridge = ridge_share * HEIGHT * WIDTH
    coeff_rows = solve_definite(gram_sum + pixel_ridge * identity_matrix, cross_sum + pixel_ridge * coefficients.T)
    frame_total = jnp.dot(coeff_rows, flat_target, precision=highest)
    frame_gram = jnp.dot(coeff_rows, coeff_rows.T, precision=highest)
    frame_ridge = ridge_share * FRAMES
    new_basis = solve_definite(frame_gram + frame_ridge * identity_matrix, frame_total + frame_ridge * flat_basis)
    return (shrunk, coeff_rows.T, new_basis.reshape(RANK, HEIGHT, WIDTH))
```

```python
import functools

import jax
import jax.numpy as jnp
from jax import lax
from jax.experimental import pallas as pl
from jax.experimental.pallas import tpu as pltpu
from jax.sharding import PartitionSpec as P

PASSES = 3


relax_rate = 0.8
smooth_weight = 0.5
smooth_floor = 0.25
shrink_level = 0.4
dual_scale = 0.8
ridge_share = 0.1


def with_halo(block, sides, width):
    for axis, dim in sides:
        count = lax.axis_size(axis)
        forward = [(i, i + 1) for i in range(count - 1)]
        backward = [(target, source) for source, target in forward]
        low = lax.ppermute(
            lax.slice_in_dim(block, block.shape[dim] - width, None, axis=dim), axis, forward
        )
        high = lax.ppermute(lax.slice_in_dim(block, 0, width, axis=dim), axis, backward)
        block = jnp.concatenate([low, block, high], axis=dim)
    return block


def forward_cells(padded, direction, shape):
    starts = [0, 0, 0]
    starts[direction] = 1
    limits = [starts[axis_dim] + shape[axis_dim] for axis_dim in range(3)]
    return lax.slice(padded, starts, limits)


def descend(padded, source, anchor, extent):
    shape = tuple((int(length) - 1 for length in padded.shape))
    here_cells = padded[:-1, :-1, :-1]
    slopes = []
    for direction in range(3):
        ahead_cells = forward_cells(padded, direction, shape)
        places = anchor[direction] + jnp.arange(shape[direction], dtype=jnp.int32)
        inside = (places >= 0) & (places < extent[direction] - 1)
        layout = [1, 1, 1]
        layout[direction] = shape[direction]
        inside = inside.reshape(layout)
        slopes.append(jnp.where(inside, ahead_cells - here_cells, jnp.zeros_like(here_cells)))
    weight = lax.rsqrt(
        smooth_floor + slopes[0] * slopes[0] + slopes[1] * slopes[1] + slopes[2] * slopes[2]
    )
    fluxes = [slope_part * weight for slope_part in slopes]
    spread = (
        fluxes[0][1:, 1:, 1:]
        - fluxes[0][:-1, 1:, 1:]
        + (fluxes[1][1:, 1:, 1:] - fluxes[1][1:, :-1, 1:])
        + (fluxes[2][1:, 1:, 1:] - fluxes[2][1:, 1:, :-1])
    )
    center = padded[1:-1, 1:-1, 1:-1]
    return center + relax_rate * (source - center + smooth_weight * spread)


HIGHEST = lax.Precision.HIGHEST


def iota(shape, dim):
    return lax.broadcasted_iota(jnp.int32, shape, dim)


def dot(a, b):
    return jnp.dot(a, b, precision=HIGHEST, preferred_element_type=jnp.float32)


def eliminated(matrix):
    n = matrix.shape[0]
    wide = (n, 128)
    lanes, rows = iota(wide, 1), iota(wide, 0)
    work = jnp.concatenate([matrix, jnp.zeros((n, 128 - n), jnp.float32)], axis=1)
    work = work + jnp.where(lanes == rows + n, 1.0, 0.0)
    for k in range(n):
        column = jnp.broadcast_to(work[:, k : k + 1], wide)
        pivot = jnp.broadcast_to(work[k : k + 1, :], wide)
        scaled = pivot / jnp.broadcast_to(column[k : k + 1, :], wide)
        work = jnp.where(rows == k, scaled, work - column * scaled)
    return work[:, n : 2 * n]


def spread_ranks(rank, width):
    return jnp.where(iota((width, rank), 0) % rank == iota((width, rank), 1), 1.0, 0.0)


def inverse_kernel(ridge, gram_ref, out_ref):
    rank = gram_ref.shape[0]
    eye = jnp.where(iota((rank, rank), 0) == iota((rank, rank), 1), ridge, 0.0)
    inverse = eliminated(gram_ref[...] + eye)
    out_ref[...] = spread_blocks(inverse, out_ref.shape[0], 4)


def spread_blocks(block, width, count):
    rank = block.shape[0]
    pick = spread_ranks(rank, width)
    full = dot(dot(pick, block), pick.T)
    a, b = iota((width, width), 0) // rank, iota((width, width), 1) // rank
    return jnp.where((a == b) & (a < count), full, 0.0)


def final_kernel(ridge, rank, slot_ref, got_ref, cross_ref, inverse_ref, old_ref, basis_ref, coeff_ref, coeff_all, stage):
    slots = got_ref.shape[0]
    rows_owned = old_ref.shape[0]
    cross = cross_ref[0]
    for peer in range(1, cross_ref.shape[0]):
        cross = cross + cross_ref[peer]
    coeff = dot(cross, inverse_ref[...])
    coeff_all[...] = coeff
    mine = coeff_all[pl.ds(slot_ref[0], 1), :]
    for f in range(4):
        coeff_ref[f : f + 1, :] = mine[:, f * rank : (f + 1) * rank]
    width = 128
    coeff_t = coeff.T
    full = dot(coeff_t, coeff)
    a, b = iota((width, width), 0) // rank, iota((width, width), 1) // rank
    pick = spread_ranks(rank, width)
    gram = dot(dot(pick.T, jnp.where(a == b, full, 0.0)), pick)
    eye = jnp.where(iota((rank, rank), 0) == iota((rank, rank), 1), ridge, 0.0)
    inverse = eliminated(gram + eye)
    lines = 8 * slots
    repeat = jnp.where(iota((slots, lines), 0) == iota((slots, lines), 1) // 8, 1.0, 0.0)
    wide = dot(coeff_t, repeat)
    wide = jnp.where(
        iota((width, lines), 0) // rank == iota((width, lines), 1) % 4, wide, 0.0
    )
    twice = spread_ranks(rank, 2 * rank)
    mix = dot(dot(twice, inverse), pick.T)
    factor = jnp.where(
        iota((2 * rank, lines), 0) // rank == (iota((2 * rank, lines), 1) // 4) % 2, dot(mix, wide), 0.0
    )
    old_factor = ridge * spread_blocks(inverse, 2 * rank, 2)
    for i in range(rows_owned):
        block = got_ref[:, 8 * i : 8 * (i + 1), :].reshape(lines, 128)
        stage[i] = dot(factor, block) + dot(old_factor, old_ref[i])
    flat = stage.reshape(rows_owned * 2 * rank, 128)
    for half in range(2):
        for r in range(rank):
            basis_ref[r, :, half * 128 : (half + 1) * 128] = flat[
                pl.ds(half * rank + r, rows_owned, stride=2 * rank), :
            ]


def vmem(count):
    return [pl.BlockSpec(memory_space=pltpu.VMEM)] * count


def local(video, multiplier, foreground, basis, coefficients):
    highest = lax.Precision.HIGHEST
    frames_here, rows_here, cols_here = video.shape
    rank_size = basis.shape[0]
    frame_count = lax.axis_size("frame")
    row_count = lax.axis_size("row")
    col_count = lax.axis_size("col")
    extent = (frames_here * frame_count, rows_here * row_count, cols_here * col_count)
    frame_slot = lax.axis_index("frame")
    corner = (
        frame_slot * frames_here,
        lax.axis_index("row") * rows_here,
        lax.axis_index("col") * cols_here,
    )
    pixels = rows_here * cols_here
    flat_basis = basis.reshape(rank_size, pixels)
    background = jnp.dot(coefficients, flat_basis, precision=highest).reshape(video.shape)
    target = video - background + dual_scale * multiplier
    blocks = row_count * col_count
    pixel_ridge = ridge_share * pixels * blocks
    gram_sum = lax.psum(jnp.dot(flat_basis, flat_basis.T, precision=highest), ("row", "col"))
    inverse = pl.pallas_call(
        functools.partial(inverse_kernel, pixel_ridge),
        out_shape=jax.ShapeDtypeStruct((128, 128), jnp.float32),
        in_specs=vmem(1),
        out_specs=vmem(1)[0],
        name="inverse",
    )(gram_sum)
    current = foreground
    for sweep in range(PASSES):
        padded = with_halo(current, (("row", 1), ("col", 2), ("frame", 0)), 1)
        current = descend(padded, target, tuple((start_cell - 1 for start_cell in corner)), extent)
        if sweep == 1:
            current, inverse = lax.optimization_barrier((current, inverse))
    shrunk = current - jnp.clip(current, -shrink_level, shrink_level)
    residual_target = video + dual_scale * multiplier - shrunk
    flat_target = residual_target.reshape(frames_here, pixels)
    cross_part = jnp.dot(flat_target, flat_basis.T, precision=highest)
    cross_part = cross_part + (pixel_ridge / blocks) * coefficients
    owned_rows = rows_here // frame_count
    chunks = residual_target.reshape(frames_here, frame_count, owned_rows, 2, 128)
    chunks = chunks.transpose(1, 2, 3, 0, 4).reshape(frame_count, owned_rows * 8, 128)
    extra = jnp.pad(cross_part.reshape(1, 1, -1), ((0, 0), (0, 7), (0, 64)))
    extra = jnp.broadcast_to(extra, (frame_count, 8, 128))
    sent = jnp.concatenate([chunks, extra], axis=1)
    got = lax.all_to_all(sent, "frame", 0, 0, tiled=True)
    cross_all = got[:, owned_rows * 8, :]
    cross_all = lax.all_to_all(
        jnp.broadcast_to(cross_all[None], (blocks, *cross_all.shape)), ("row", "col"), 0, 0, tiled=True
    )
    old_owned = lax.dynamic_slice_in_dim(basis, frame_slot * owned_rows, owned_rows, 1)
    old_owned = old_owned.reshape(rank_size, owned_rows, 2, 128).transpose(1, 2, 0, 3)
    old_owned = old_owned.reshape(owned_rows, 2 * rank_size, 128)
    frame_ridge = ridge_share * frames_here * frame_count
    new_basis, new_coeff = pl.pallas_call(
        functools.partial(final_kernel, frame_ridge, rank_size),
        out_shape=(
            jax.ShapeDtypeStruct((rank_size, owned_rows, cols_here), jnp.float32),
            jax.ShapeDtypeStruct((frames_here, rank_size), jnp.float32),
        ),
        in_specs=[pl.BlockSpec(memory_space=pltpu.SMEM)] + vmem(4),
        out_specs=vmem(2),
        scratch_shapes=[
            pltpu.VMEM((frame_count, 128), jnp.float32),
            pltpu.VMEM((owned_rows, 2 * rank_size, 128), jnp.float32),
        ],
        name="final",
    )(frame_slot.reshape(1), got, cross_all, inverse, old_owned)
    return shrunk, new_coeff, new_basis


def solution(mesh):
    placed = (
        P("frame", "row", "col"),
        P("frame", "row", "col"),
        P("frame", "row", "col"),
        P(None, "row", "col"),
        P("frame", None),
    )
    return jax.shard_map(
        local,
        mesh=mesh,
        in_specs=placed,
        out_specs=(P("frame", "row", "col"), P("frame", None), P(None, ("row", "frame"), "col")),
        check_vma=False,
    )
```

```python
import functools

import jax
import jax.numpy as jnp
from jax import lax
from jax.experimental import pallas as pl
from jax.experimental.pallas import tpu as pltpu
from jax.sharding import PartitionSpec as P

PASSES = 3


relax_rate = 0.8
smooth_weight = 0.5
smooth_floor = 0.25
shrink_level = 0.4
dual_scale = 0.8
ridge_share = 0.1


HIGHEST = lax.Precision.HIGHEST


def iota(shape, dim):
    return lax.broadcasted_iota(jnp.int32, shape, dim)


def dot(a, b):
    return jnp.dot(a, b, precision=HIGHEST, preferred_element_type=jnp.float32)


def eliminated(matrix):
    n = matrix.shape[0]
    wide = (n, 128)
    lanes, rows = iota(wide, 1), iota(wide, 0)
    work = jnp.concatenate([matrix, jnp.zeros((n, 128 - n), jnp.float32)], axis=1)
    work = work + jnp.where(lanes == rows + n, 1.0, 0.0)
    for k in range(n):
        column = jnp.broadcast_to(work[:, k : k + 1], wide)
        pivot = jnp.broadcast_to(work[k : k + 1, :], wide)
        scaled = pivot / jnp.broadcast_to(column[k : k + 1, :], wide)
        work = jnp.where(rows == k, scaled, work - column * scaled)
    return work[:, n : 2 * n]


def spread_ranks(rank, width):
    return jnp.where(iota((width, rank), 0) % rank == iota((width, rank), 1), 1.0, 0.0)


def spread_blocks(block, width, count):
    rank = block.shape[0]
    pick = spread_ranks(rank, width)
    full = dot(dot(pick, block), pick.T)
    a, b = iota((width, width), 0) // rank, iota((width, width), 1) // rank
    return jnp.where((a == b) & (a < count), full, 0.0)


def final_kernel(pixel_ridge, ridge, slot_ref, got_ref, parts_ref, old_ref, basis_ref, coeff_ref, coeff_all):
    slots = got_ref.shape[0]
    rows_owned = old_ref.shape[0]
    rank = basis_ref.shape[1]
    total = parts_ref[0]
    for peer in range(1, parts_ref.shape[0]):
        total = total + parts_ref[peer]
    eye = jnp.where(iota((rank, rank), 0) == iota((rank, rank), 1), 1.0, 0.0)
    inverse = eliminated(total[slots:, 0:rank] + pixel_ridge * eye)
    coeff = dot(total[0:slots], spread_blocks(inverse, 128, 4))
    coeff_all[...] = coeff
    mine = coeff_all[pl.ds(slot_ref[0], 1), :]
    for f in range(4):
        coeff_ref[f : f + 1, :] = mine[:, f * rank : (f + 1) * rank]
    width = 128
    coeff_t = coeff.T
    full = dot(coeff_t, coeff)
    a, b = iota((width, width), 0) // rank, iota((width, width), 1) // rank
    pick = spread_ranks(rank, width)
    gram = dot(dot(pick.T, jnp.where(a == b, full, 0.0)), pick)
    inverse = eliminated(gram + ridge * eye)
    lines = 8 * slots
    repeat = jnp.where(iota((slots, lines), 0) == iota((slots, lines), 1) // 8, 1.0, 0.0)
    wide = dot(coeff_t, repeat)
    wide = jnp.where(
        iota((width, lines), 0) // rank == iota((width, lines), 1) % 4, wide, 0.0
    )
    twice = spread_ranks(rank, 2 * rank)
    mix = dot(dot(twice, inverse), pick.T)
    factor = jnp.where(
        iota((2 * rank, lines), 0) // rank == (iota((2 * rank, lines), 1) // 4) % 2, dot(mix, wide), 0.0
    )
    old_factor = ridge * spread_blocks(inverse, 2 * rank, 2)
    for i in range(rows_owned):
        block = got_ref[:, 8 * i : 8 * (i + 1), :].reshape(lines, 128)
        rows = dot(factor, block) + dot(old_factor, old_ref[i])
        for half in range(2):
            basis_ref[i, :, half * 128 : (half + 1) * 128] = rows[half * rank : (half + 1) * rank]


HALO = 3
GROUP = 12
TOP = 8
FLOOR, SMOOTH, RELAX = smooth_floor, smooth_weight, relax_rate


def lane_of(rows):
    return iota((rows, 128), 1)


def in_lanes(lanes, first, count):
    first = first % 128
    if first + count <= 128:
        return (lanes >= first) & (lanes < first + count)
    return (lanes >= first) | (lanes < first + count - 128)


def goal_rows(coeff, video, multiplier, basis, at):
    frames, rank = video.shape[0], basis.shape[0]
    sums = [None] * frames
    for r in range(rank):
        image = basis[r, at, :]
        for f in range(frames):
            term = coeff[f, r] * image
            sums[f] = term if r == 0 else sums[f] + term
    return [video[f, at, :] - sums[f] + dual_scale * multiplier[f, at, :] for f in range(frames)]


def edge_kernel(place, coeff, video, multiplier, basis, current, edge, *scratch):
    buffers, sems = scratch[:-1], scratch[-1]
    frames, rows, _ = video.shape
    at = pl.ds(pl.multiple_of((1 - place[0]) * (rows - 8), 8), 8)
    near = [
        pltpu.make_async_copy(ref.at[:, at, :], buf, sems.at[k])
        for k, (ref, buf) in enumerate(zip((video, multiplier, basis, current), buffers))
    ]
    for c in near:
        c.start()
    for c in near:
        c.wait()
    video, multiplier, basis, current = buffers
    edge[0] = current[...]
    for f, value in enumerate(goal_rows(coeff, video, multiplier, basis, slice(0, 8))):
        edge[1, f] = value


def target_kernel(
    coeff, video_in, multiplier_in, basis_in, current, up, down, video, multiplier, basis, low, high, sems
):
    frames, rows, _ = video.shape
    pieces, chunk = sems.shape[1], 16
    piece = rows // pieces
    waits = []
    for p in range(pieces):
        at = pl.ds(p * piece, piece)
        for k, (ref, buf) in enumerate(((basis_in, basis), (video_in, video), (multiplier_in, multiplier))):
            c = pltpu.make_async_copy(ref.at[:, at, :], buf.at[:, at, :], sems.at[k, p])
            c.start()
            waits.append(c)
    outs = [
        pltpu.make_async_copy(current.at[pl.ds(frames - HALO, HALO)], up.at[pl.ds(0, HALO)], sems.at[5, 0]),
        pltpu.make_async_copy(current.at[pl.ds(0, HALO)], down.at[pl.ds(0, HALO)], sems.at[5, 1]),
    ]
    for c in outs:
        c.start()
    for p in range(pieces):
        for c in waits[3 * p : 3 * p + 3]:
            c.wait()

        def body(c, carry):
            at = pl.ds(pl.multiple_of(p * piece + c * chunk, chunk), chunk)
            goals = goal_rows(coeff, video, multiplier, basis, at)
            for f in range(frames):
                (low if f < 2 else high)[f % 2, at, :] = goals[f]
            return carry

        lax.fori_loop(0, piece // chunk, body, 0)
        at = pl.ds(p * piece, piece)
        for k, (buf, ref) in enumerate(((low, down), (high, up))):
            c = pltpu.make_async_copy(buf.at[:, at, :], ref.at[pl.ds(HALO, 2), at, :], sems.at[3 + k, p])
            c.start()
            outs.append(c)
    for c in outs:
        c.wait()


def strips_kernel(current, up, down, edge, right, left):
    frames, rows, _ = current.shape
    sources = [(current, f, HALO * GROUP + GROUP * f, 0, f) for f in range(frames)]
    sources += [
        (down if f < 2 else up, HALO + f % 2, HALO * GROUP + GROUP * (f + frames), 1, f) for f in range(frames)
    ]

    def gather(out_at, count, pick):
        lanes = lane_of(count)
        a = jnp.zeros((count, 128), jnp.float32)
        b = a
        for ref, index, base, kind, f in sources:
            first, last = pick(ref, index, kind, f)
            both = jnp.where(lanes < 64, first, last)
            here = in_lanes(lanes, base, GROUP)
            a = jnp.where(here, pltpu.roll(both, (base + 3) % 128, 1), a)
            b = jnp.where(here, pltpu.roll(both, (base + 8) % 128, 1), b)
        right[out_at, :] = a
        left[out_at, :] = b

    def body(c, carry):
        at = pl.ds(pl.multiple_of(c * 32, 32), 32)
        out_at = pl.ds(pl.multiple_of(c * 32 + TOP, 8), 32)
        gather(out_at, 32, lambda ref, i, kind, f: (ref[i, at, 0:128], ref[i, at, 128:256]))
        return carry

    lax.fori_loop(0, rows // 32, body, 0)
    for out_at in (pl.ds(0, 8), pl.ds(rows + TOP, 8)):
        gather(out_at, 8, lambda ref, i, kind, f: (edge[kind, f, :, 0:128], edge[kind, f, :, 128:256]))


def ring_kernel(right, left, from_left, from_right, edge, out):
    rows = right.shape[0]
    lanes = lane_of(rows)
    k = (lanes + 128 - HALO * GROUP) % 128 % GROUP
    out[0:rows, :] = jnp.where(
        k <= 2,
        from_left[...],
        jnp.where(k <= 5, right[...], jnp.where(k <= 7, left[...], from_right[...])),
    )
    flat = edge.reshape(edge.shape[0] * edge.shape[1] * 8, 256)
    for half in range(2):
        at = rows + half * flat.shape[0]
        out[at : at + flat.shape[0], :] = flat[:, half * 128 : (half + 1) * 128]


def sweep_kernel(
    ridge_part,
    slot_count,
    col_count,
    place,
    current,
    before,
    after,
    up,
    down,
    ring,
    ring_before,
    ring_after,
    video,
    multiplier,
    basis,
    coeff,
    shrunk_out,
    sent,
    s_a,
    s_b,
    goal,
    strip_a,
    strip_b,
    strip_goal,
    strip_flux,
    flux_f,
    own_video,
    own_multiplier,
    own_basis,
    residual,
    out,
    sums,
    sems,
):
    frames, rows, _ = current.shape
    all_rows = rows + 2 * TOP
    rank = basis.shape[0]
    row, col, slot = place[0], place[1], place[2]
    copies = []

    def copy(src, dst):
        c = pltpu.make_async_copy(src, dst, sems.at[len(copies)])
        c.start()
        copies.append(c)
        return c

    own_at = pl.ds(TOP, rows)
    strip_chunks = [(c, min(80, all_rows - c)) for c in range(0, all_rows, 80)]
    first = []
    for half in range(2):
        at = pl.ds(half * 128, 128)
        for src, at_frame, count in ((before, 0, HALO), (current, HALO, frames), (after, HALO + frames, HALO)):
            first.append(copy(src.at[pl.ds(0, count), :, at], s_a.at[pl.ds(at_frame, count), half, own_at, :]))
        for src, at_frame in ((before, 0), (down, 2), (up, 4), (after, 6)):
            first.append(copy(src.at[pl.ds(HALO, 2), :, at], goal.at[pl.ds(at_frame, 2), half, own_at, :]))
    later = [copy(video, own_video), copy(multiplier, own_multiplier), copy(basis, own_basis)]

    for c, count in strip_chunks:
        at = slice(c, c + count)
        lanes = lane_of(count)
        mine, prev, nxt = ring[at, :], ring_before[at, :], ring_after[at, :]
        strip_a[at, :] = jnp.where(
            lanes < 36, pltpu.roll(prev, 80, 1), jnp.where(lanes < 84, mine, pltpu.roll(nxt, 48, 1))
        )
        strip_goal[at, :] = jnp.where(
            lanes < 36, pltpu.roll(prev, 32, 1), jnp.where(lanes < 84, pltpu.roll(mine, 80, 1), nxt)
        )
    zero8 = jnp.zeros((8, 128), jnp.float32)
    for buf in (strip_a, strip_b):
        buf[pl.ds(all_rows, 8), :] = zero8
    for half in range(2):
        for g in range(2 * HALO + frames):
            if g < HALO:
                src, f = ring_before, g + 1
            elif g < HALO + frames:
                src, f = ring, g - HALO
            else:
                src, f = ring_after, g - HALO - frames
            base = all_rows + half * 64
            tile = src[base + 8 * f : base + 8 * f + 8, :]
            s_a[g, half, 0:TOP, :] = tile
            s_a[g, half, pl.ds(TOP + rows, 8), :] = tile
            s_a[g, half, pl.ds(all_rows, 8), :] = zero8
            s_b[g, half, pl.ds(all_rows, 8), :] = zero8
            if 1 <= g <= 2 * HALO + frames - 2:
                tile = src[base + 32 + 8 * f : base + 32 + 8 * f + 8, :]
                goal[g - 1, half, 0:TOP, :] = tile
                goal[g - 1, half, pl.ds(TOP + rows, 8), :] = tile

    def first_row_last(value, count):
        return value[count - 1 : count, :]

    def down_one(value, carry, count):
        moved = pltpu.roll(value, 1, 0)
        return jnp.where(iota((count, 128), 0) == 0, jnp.broadcast_to(carry, (count, 128)), moved)

    def strip_sweep(old, new, flux_at):
        for c, count in strip_chunks:
            lanes = lane_of(count)
            k = lanes % GROUP
            s = old[c : c + count, :]
            s = jnp.where((slot == 0) & in_lanes(lanes, 24, 12), pltpu.roll(s, 116, 1), s)
            s = jnp.where((slot == slots_end) & in_lanes(lanes, 84, 12), pltpu.roll(s, 12, 1), s)
            s = jnp.where((col == 0) & (k == 2), pltpu.roll(s, 127, 1), s)
            s = jnp.where((col == cols_end) & (k == 8), pltpu.roll(s, 1, 1), s)
            old[c : c + count, :] = s

        @pl.when(row == 0)
        def _():
            old[TOP - 1 : TOP, :] = old[TOP : TOP + 1, :]

        @pl.when(row == 1)
        def _():
            old[TOP + rows : TOP + rows + 1, :] = old[TOP + rows - 1 : TOP + rows, :]

        carry = jnp.zeros((1, 128), jnp.float32)
        for c, count in strip_chunks:
            s = old[c : c + count, :]
            pf = pltpu.roll(s, 116, 1) - s
            pr = old[c + 1 : c + 1 + count, :] - s
            pc = pltpu.roll(s, 127, 1) - s
            weight = lax.rsqrt(FLOOR + pf * pf + pr * pr + pc * pc)
            ff, fr, fc = pf * weight, pr * weight, pc * weight
            strip_flux[flux_at, c : c + count, :] = fc
            spread = (
                (ff - pltpu.roll(ff, 12, 1)) + (fr - down_one(fr, carry, count)) + (fc - pltpu.roll(fc, 1, 1))
            )
            carry = first_row_last(fr, count)
            new[c : c + count, :] = s + RELAX * (strip_goal[c : c + count, :] - s + SMOOTH * spread)

    slots_end, cols_end = slot_count - 1, col_count - 1
    strip_sweep(strip_a, strip_b, 0)

    for c in first:
        c.wait()

    chunks = [(c, min(32, all_rows - c)) for c in range(0, all_rows, 32)]

    def edges(old):
        @pl.when(slot == 0)
        def _():
            old[HALO - 1] = old[HALO]

        @pl.when(slot == slots_end)
        def _():
            old[HALO + frames] = old[HALO + frames - 1]

        @pl.when(row == 0)
        def _():
            for g in range(2 * HALO + frames):
                for half in range(2):
                    old[g, half, TOP - 1 : TOP, :] = old[g, half, TOP : TOP + 1, :]

        @pl.when(row == 1)
        def _():
            end = TOP + rows
            for g in range(2 * HALO + frames):
                for half in range(2):
                    old[g, half, end : end + 1, :] = old[g, half, end - 1 : end, :]

    last_keep = jnp.where((lane_of(8)[0:1] == 127) & (col == cols_end), 0.0, 1.0)

    def main_sweep(old, new, strip, flux_at, g_first, g_count):
        edges(old)

        def body(i, carry0):
            g = g_first + i
            turn_ahead = (119 + 12 * 128 - 12 * g) % 128
            turn_flux = (128 * 12 - 2 - 12 * g) % 128
            goal_at = jnp.maximum(g - 1, 0)
            carry = [jnp.zeros((1, 128), jnp.float32)] * 2
            for c, count in chunks:
                lanes = lane_of(count)
                at = pl.ds(c, count)
                next_at = pl.ds(c + 1, count)
                s = [old[g, half, at, :] for half in range(2)]
                turned = [pltpu.roll(x, 127, 1) for x in s]
                outside = pltpu.roll(strip[at, :], turn_ahead, 1)
                ahead = [
                    jnp.where(lanes == 127, turned[1], turned[0]),
                    jnp.where(lanes == 127, outside, turned[1]),
                ]
                fc, fr, ff = [], [], []
                for half in range(2):
                    x = s[half]
                    pf = old[g + 1, half, at, :] - x
                    pr = old[g, half, next_at, :] - x
                    pc = ahead[half] - x
                    if half == 1:
                        pc = pc * last_keep
                    weight = lax.rsqrt(FLOOR + pf * pf + pr * pr + pc * pc)
                    ff.append(pf * weight)
                    fr.append(pr * weight)
                    fc.append(pc * weight)
                outside = pltpu.roll(strip_flux[flux_at, at, :], turn_flux, 1)
                turned = [pltpu.roll(x, 1, 1) for x in fc]
                behind = [
                    jnp.where(lanes == 0, outside, turned[0]),
                    jnp.where(lanes == 0, turned[0], turned[1]),
                ]
                for half in range(2):
                    x = s[half]
                    spread = (
                        (ff[half] - flux_f[half, at, :])
                        + (fr[half] - down_one(fr[half], carry[half], count))
                        + (fc[half] - behind[half])
                    )
                    flux_f[half, at, :] = ff[half]
                    new[g, half, at, :] = x + RELAX * (goal[goal_at, half, at, :] - x + SMOOTH * spread)
                carry = [first_row_last(x, count) for x in fr]
            return carry0

        lax.fori_loop(0, g_count, body, 0)

    main_sweep(s_a, s_b, strip_a, 0, 0, 9)
    strip_sweep(strip_b, strip_a, 1)
    main_sweep(s_b, s_a, strip_b, 1, 1, 7)
    strip_sweep(strip_a, strip_b, 2)
    main_sweep(s_a, s_b, strip_a, 2, 2, 5)

    for c in later:
        c.wait()
    sums[...] = jnp.zeros_like(sums)

    def finish(c, carry):
        chunk = 16
        at = pl.ds(pl.multiple_of(c * chunk, chunk), chunk)
        in_at = pl.ds(pl.multiple_of(c * chunk + TOP, 8), chunk)
        parts = []
        for f in range(frames):
            for half in range(2):
                cols = slice(half * 128, (half + 1) * 128)
                s = s_b[HALO + f, half, in_at, :]
                shrunk = s - jnp.clip(s, -shrink_level, shrink_level)
                out[f, at, cols] = shrunk
                r = own_video[f, at, cols] + dual_scale * own_multiplier[f, at, cols] - shrunk
                residual[half * frames + f, at, :] = r
                parts.append(r)
        for r in range(rank):
            images = [own_basis[r, at, half * 128 : (half + 1) * 128] for half in range(2)]
            for f in range(frames):
                term = images[0] * parts[2 * f] + images[1] * parts[2 * f + 1]
                sums[f * rank + r] += term[0:8] + term[8:16]
        return carry

    lax.fori_loop(0, rows // 16, finish, 0)
    done = copy(out, shrunk_out)
    lines = jnp.sum(sums[...], axis=1)
    total = lax.dot_general(
        jnp.ones((8, 128), jnp.float32),
        lines,
        (((1,), (1,)), ((), ())),
        precision=HIGHEST,
        preferred_element_type=jnp.float32,
    )
    cross = jnp.concatenate([total + ridge_part * coeff[...], jnp.zeros((8, 64), jnp.float32)], axis=1)
    chunk_rows = sent.shape[1]
    owned = rows // slot_count
    flat = sent.reshape(sent.shape[0] * chunk_rows, 128)

    def pack(j, carry):
        for f in range(frames):
            for half in range(2):
                flat[pl.ds(j * chunk_rows + half * frames + f, owned, stride=8), :] = residual[
                    half * frames + f, pl.ds(j * owned, owned), :
                ]
        sent[j, pl.ds(owned * 8, 8), :] = cross
        return carry

    lax.fori_loop(0, slot_count, pack, 0)
    done.wait()


def gram_kernel(slot, basis, out, old, sums, window):
    rank, rows, _ = basis.shape
    sums[...] = jnp.zeros_like(sums)

    def body(c, carry):
        at = pl.ds(pl.multiple_of(c * 8, 8), 8)
        images = [[basis[r, at, half * 128 : (half + 1) * 128] for half in range(2)] for r in range(rank)]
        for r in range(rank):
            for q in range(r, rank):
                sums[r * rank + q] += images[r][0] * images[q][0] + images[r][1] * images[q][1]
        return carry

    lax.fori_loop(0, rows // 8, body, 0)
    owned = old.shape[0]
    start = pl.multiple_of(slot[0] * owned // 8 * 8, 8)
    shift = slot[0] * owned - start
    flat = old.reshape(owned * 2 * rank, 128)
    for half in range(2):
        for r in range(rank):
            window[half * rank + r] = basis[r, pl.ds(start, 16), half * 128 : (half + 1) * 128]
            flat[pl.ds(half * rank + r, owned, stride=2 * rank), :] = window[half * rank + r, pl.ds(shift, owned), :]
    ones = jnp.ones((128, 128), jnp.float32)
    for r in range(rank):
        lines = jnp.concatenate(
            [jnp.sum(sums[min(r, q) * rank + max(r, q)], axis=0, keepdims=True) for q in range(rank)], axis=0
        )
        totals = dot(lines, ones)
        picked = jnp.where(iota((rank, 128), 0) == iota((rank, 128), 1), totals, 0.0)
        out[r : r + 1, :] = jnp.sum(picked, axis=0, keepdims=True)


def vmem(count):
    return [pl.BlockSpec(memory_space=pltpu.VMEM)] * count


def smem():
    return pl.BlockSpec(memory_space=pltpu.SMEM)


def anywhere(count):
    return [pl.BlockSpec(memory_space=pltpu.HBM)] * count


def floats(*shape):
    return jax.ShapeDtypeStruct(shape, jnp.float32)


LARGE = pltpu.CompilerParams(vmem_limit_bytes=48 * 1024 * 1024)


def local(video, multiplier, foreground, basis, coefficients):
    frames, rows, cols = video.shape
    rank = basis.shape[0]
    frame_count = lax.axis_size("frame")
    row_count = lax.axis_size("row")
    col_count = lax.axis_size("col")
    blocks = row_count * col_count
    frame_slot = lax.axis_index("frame")
    place = jnp.stack([lax.axis_index("row"), lax.axis_index("col"), frame_slot])
    all_rows = rows + 2 * TOP
    to_next = [(i, i + 1) for i in range(frame_count - 1)]
    to_previous = [(b, a) for a, b in to_next]
    to_right = [(i, i + 1) for i in range(col_count - 1)]
    to_left = [(b, a) for a, b in to_right]

    edge = pl.pallas_call(
        edge_kernel,
        out_shape=floats(2, frames, 8, cols),
        in_specs=[smem(), smem()] + anywhere(4),
        out_specs=vmem(1)[0],
        scratch_shapes=[pltpu.VMEM((n, 8, cols), jnp.float32) for n in (frames, frames, rank, frames)]
        + [pltpu.SemaphoreType.DMA((4,))],
        name="edge",
    )(place, coefficients, video, multiplier, basis, foreground)
    edge = lax.ppermute(edge, "row", [(0, 1), (1, 0)])
    up, down = pl.pallas_call(
        target_kernel,
        out_shape=(floats(HALO + 2, rows, cols), floats(HALO + 2, rows, cols)),
        in_specs=[smem()] + anywhere(4),
        out_specs=anywhere(2),
        scratch_shapes=[pltpu.VMEM(s, jnp.float32) for s in (video.shape, video.shape, basis.shape)]
        + [pltpu.VMEM((2, rows, cols), jnp.float32)] * 2
        + [pltpu.SemaphoreType.DMA((6, 6))],
        compiler_params=LARGE,
        name="target",
    )(coefficients, video, multiplier, basis, foreground)
    up, down, edge = lax.optimization_barrier((up, down, edge))
    before = lax.ppermute(up, "frame", to_next)
    after = lax.ppermute(down, "frame", to_previous)
    right, left = pl.pallas_call(
        strips_kernel,
        out_shape=(floats(all_rows, 128), floats(all_rows, 128)),
        in_specs=vmem(4),
        out_specs=vmem(2),
        compiler_params=LARGE,
        name="strips",
    )(foreground, up, down, edge)
    from_left = lax.ppermute(right, "col", to_right)
    from_right = lax.ppermute(left, "col", to_left)
    ring = pl.pallas_call(
        ring_kernel,
        out_shape=floats(all_rows + 128, 128),
        in_specs=vmem(5),
        out_specs=vmem(1)[0],
        compiler_params=LARGE,
        name="ring",
    )(right, left, from_left, from_right, edge)
    ring_before = lax.ppermute(ring, "frame", to_next)
    ring_after = lax.ppermute(ring, "frame", to_previous)

    pixel_ridge = ridge_share * rows * cols * blocks
    owned_rows = rows // frame_count
    main = (2 * HALO + frames, 2, all_rows + 8, 128)
    strip = (all_rows + 8, 128)
    scratch = [
        main,
        main,
        (2 * HALO + frames - 2, 2, all_rows, 128),
        strip,
        strip,
        (all_rows, 128),
        (3, all_rows, 128),
        (2, all_rows, 128),
        video.shape,
        video.shape,
        basis.shape,
        (2 * frames, rows, 128),
        video.shape,
        (frames * rank, 8, 128),
    ]
    shrunk, sent = pl.pallas_call(
        functools.partial(sweep_kernel, pixel_ridge / blocks, frame_count, col_count),
        out_shape=(floats(frames, rows, cols), floats(frame_count, owned_rows * 8 + 8, 128)),
        in_specs=[smem()] + anywhere(5) + vmem(3) + anywhere(3) + vmem(1),
        out_specs=anywhere(1) + vmem(1),
        scratch_shapes=[pltpu.VMEM(s, jnp.float32) for s in scratch] + [pltpu.SemaphoreType.DMA((18,))],
        compiler_params=LARGE,
        name="sweeps",
    )(
        place,
        foreground,
        before,
        after,
        up,
        down,
        ring,
        ring_before,
        ring_after,
        video,
        multiplier,
        basis,
        coefficients.reshape(1, frames * rank),
    )
    got = lax.all_to_all(sent, "frame", 0, 0, tiled=True)
    basis, _ = lax.optimization_barrier((basis, sent))
    gram, old_owned = pl.pallas_call(
        gram_kernel,
        out_shape=(floats(rank, 128), floats(owned_rows, 2 * rank, 128)),
        in_specs=[smem()] + vmem(1),
        out_specs=vmem(2),
        scratch_shapes=[
            pltpu.VMEM((rank * rank, 8, 128), jnp.float32),
            pltpu.VMEM((2 * rank, 16, 128), jnp.float32),
        ],
        compiler_params=LARGE,
        name="gram",
    )(frame_slot.reshape(1), basis)
    parts = jnp.concatenate([got[:, owned_rows * 8, :], gram], axis=0)
    parts = lax.all_to_all(jnp.broadcast_to(parts[None], (blocks, *parts.shape)), ("row", "col"), 0, 0, tiled=True)
    frame_ridge = ridge_share * frames * frame_count
    new_basis, new_coeff = pl.pallas_call(
        functools.partial(final_kernel, pixel_ridge, frame_ridge),
        out_shape=(floats(owned_rows, rank, cols), floats(frames, rank)),
        in_specs=[smem()] + vmem(3),
        out_specs=vmem(2),
        scratch_shapes=[pltpu.VMEM((frame_count, 128), jnp.float32)],
        compiler_params=LARGE,
        name="final",
    )(frame_slot.reshape(1), got, parts, old_owned)
    return shrunk, new_coeff, new_basis.transpose(1, 0, 2)


def solution(mesh):
    placed = (
        P("frame", "row", "col"),
        P("frame", "row", "col"),
        P("frame", "row", "col"),
        P(None, "row", "col"),
        P("frame", None),
    )
    return jax.shard_map(
        local,
        mesh=mesh,
        in_specs=placed,
        out_specs=(P("frame", "row", "col"), P("frame", None), P(None, ("row", "frame"), "col")),
        check_vma=False,
    )
```

```python
import functools

import jax
import jax.numpy as jnp
from jax import lax
from jax.experimental import pallas as pl
from jax.experimental.pallas import tpu as pltpu
from jax.sharding import PartitionSpec as P

PASSES = 3


relax_rate = 0.8
smooth_weight = 0.5
smooth_floor = 0.25
shrink_level = 0.4
dual_scale = 0.8
ridge_share = 0.1


HIGHEST = lax.Precision.HIGHEST


def iota(shape, dim):
    return lax.broadcasted_iota(jnp.int32, shape, dim)


def dot(a, b):
    return jnp.dot(a, b, precision=HIGHEST, preferred_element_type=jnp.float32)


def eliminated(matrix):
    n = matrix.shape[0]
    wide = (n, 128)
    lanes, rows = iota(wide, 1), iota(wide, 0)
    work = jnp.concatenate([matrix, jnp.zeros((n, 128 - n), jnp.float32)], axis=1)
    work = work + jnp.where(lanes == rows + n, 1.0, 0.0)
    for k in range(0, n, 2):
        col0 = jnp.broadcast_to(work[:, k : k + 1], wide)
        col1 = jnp.broadcast_to(work[:, k + 1 : k + 2], wide)
        row0, row1 = work[k : k + 1, :], work[k + 1 : k + 2, :]
        a, b, d = col0[k : k + 1, :], col1[k : k + 1, :], col1[k + 1 : k + 2, :]
        scale = 1.0 / (a * d - b * b)
        new0 = jnp.broadcast_to((d * row0 - b * row1) * scale, wide)
        new1 = jnp.broadcast_to((a * row1 - b * row0) * scale, wide)
        left = work - col0 * new0 - col1 * new1
        work = jnp.where(rows == k, new0, jnp.where(rows == k + 1, new1, left))
    return work[:, n : 2 * n]


def spread_ranks(rank, width):
    return jnp.where(iota((width, rank), 0) % rank == iota((width, rank), 1), 1.0, 0.0)


def spread_blocks(block, width, count):
    rank = block.shape[0]
    pick = spread_ranks(rank, width)
    full = dot(dot(pick, block), pick.T)
    a, b = iota((width, width), 0) // rank, iota((width, width), 1) // rank
    return jnp.where((a == b) & (a < count), full, 0.0)


def final_kernel(pixel_ridge, ridge, slot_ref, got_ref, parts_ref, old_ref, basis_ref, coeff_ref, coeff_all):
    slots = got_ref.shape[0]
    rows_owned = old_ref.shape[0]
    rank = basis_ref.shape[1]
    total = parts_ref[0]
    for peer in range(1, parts_ref.shape[0]):
        total = total + parts_ref[peer]
    eye = jnp.where(iota((rank, rank), 0) == iota((rank, rank), 1), 1.0, 0.0)
    inverse = eliminated(total[slots:, 0:rank] + pixel_ridge * eye)
    coeff = dot(total[0:slots], spread_blocks(inverse, 128, 4))
    coeff_all[...] = coeff
    mine = coeff_all[pl.ds(slot_ref[0], 1), :]
    for f in range(4):
        coeff_ref[f : f + 1, :] = mine[:, f * rank : (f + 1) * rank]
    width = 128
    coeff_t = coeff.T
    full = dot(coeff_t, coeff)
    a, b = iota((width, width), 0) // rank, iota((width, width), 1) // rank
    pick = spread_ranks(rank, width)
    gram = dot(dot(pick.T, jnp.where(a == b, full, 0.0)), pick)
    lines = 8 * slots
    repeat = jnp.where(iota((slots, lines), 0) == iota((slots, lines), 1) // 8, 1.0, 0.0)
    wide = dot(coeff_t, repeat)
    wide = jnp.where(iota((width, lines), 0) // rank == iota((width, lines), 1) % 4, wide, 0.0)
    narrow = wide[0:rank]
    for f in range(1, 4):
        narrow = narrow + wide[f * rank : (f + 1) * rank]
    twice = jnp.concatenate([narrow, narrow], axis=0)
    factor = jnp.where(
        iota((2 * rank, lines), 0) // rank == (iota((2 * rank, lines), 1) // 4) % 2, twice, 0.0
    )
    sums = []
    for i in range(0, rows_owned):
        block = got_ref[:, 8 * i : 8 * (i + 1), :].reshape(lines, 128)
        sums.append(dot(factor, block) + ridge * old_ref[i])
    inverse = spread_blocks(eliminated(gram + ridge * eye), 2 * rank, 2)
    for i in range(rows_owned):
        rows = dot(inverse, sums[i])
        for half in range(2):
            basis_ref[i, :, half * 128 : (half + 1) * 128] = rows[half * rank : (half + 1) * rank]


HALO = 3
GROUP = 12
TOP = 8
FLOOR, SMOOTH, RELAX = smooth_floor, smooth_weight, relax_rate


def lane_of(rows):
    return iota((rows, 128), 1)


def in_lanes(lanes, first, count):
    first = first % 128
    if first + count <= 128:
        return (lanes >= first) & (lanes < first + count)
    return (lanes >= first) | (lanes < first + count - 128)


def goal_rows(coeff, video, multiplier, basis, at):
    frames, rank = video.shape[0], basis.shape[0]
    sums = [None] * frames
    for r in range(rank):
        image = basis[r, at, :]
        for f in range(frames):
            term = coeff[f, r] * image
            sums[f] = term if r == 0 else sums[f] + term
    return [video[f, at, :] - sums[f] + dual_scale * multiplier[f, at, :] for f in range(frames)]


def edge_kernel(place, coeff, video, multiplier, basis, current, edge, *scratch):
    buffers, sems = scratch[:-1], scratch[-1]
    frames, rows, _ = video.shape
    at = pl.ds(pl.multiple_of((1 - place[0]) * (rows - 8), 8), 8)
    near = [
        pltpu.make_async_copy(ref.at[:, at, :], buf, sems.at[k])
        for k, (ref, buf) in enumerate(zip((video, multiplier, basis, current), buffers))
    ]
    for c in near:
        c.start()
    for c in near:
        c.wait()
    video, multiplier, basis, current = buffers
    edge[0] = current[...]
    for f, value in enumerate(goal_rows(coeff, video, multiplier, basis, slice(0, 8))):
        edge[1, f] = value


def target_kernel(coeff, video, multiplier, basis_in, current, up, down, basis, sems):
    frames, rows, _ = video.shape
    pieces, chunk = sems.shape[0], 16
    piece = rows // pieces
    waits = []
    for p in range(pieces):
        at = pl.ds(p * piece, piece)
        waits.append(pltpu.make_async_copy(basis_in.at[:, at, :], basis.at[:, at, :], sems.at[p]))
        waits[p].start()
    for k in range(HALO):
        up[k] = current[frames - HALO + k]
        down[k] = current[k]
    for p in range(pieces):
        waits[p].wait()

        def body(c, carry):
            at = pl.ds(pl.multiple_of(p * piece + c * chunk, chunk), chunk)
            for f, value in enumerate(goal_rows(coeff, video, multiplier, basis, at)):
                (down if f < 2 else up)[HALO + f % 2, at, :] = value
            return carry

        lax.fori_loop(0, piece // chunk, body, 0)


def strips_kernel(current, up, down, edge, right, left):
    frames, rows, _ = current.shape
    sources = [(current, f, HALO * GROUP + GROUP * f, 0, f) for f in range(frames)]
    sources += [
        (down if f < 2 else up, HALO + f % 2, HALO * GROUP + GROUP * (f + frames), 1, f) for f in range(frames)
    ]

    def gather(out_at, count, pick):
        lanes = lane_of(count)
        a = jnp.zeros((count, 128), jnp.float32)
        b = a
        for ref, index, base, kind, f in sources:
            first, last = pick(ref, index, kind, f)
            both = jnp.where(lanes < 64, first, last)
            here = in_lanes(lanes, base, GROUP)
            a = jnp.where(here, pltpu.roll(both, (base + 3) % 128, 1), a)
            b = jnp.where(here, pltpu.roll(both, (base + 8) % 128, 1), b)
        right[out_at, :] = a
        left[out_at, :] = b

    def body(c, carry):
        at = pl.ds(pl.multiple_of(c * 32, 32), 32)
        out_at = pl.ds(pl.multiple_of(c * 32 + TOP, 8), 32)
        gather(out_at, 32, lambda ref, i, kind, f: (ref[i, at, 0:128], ref[i, at, 128:256]))
        return carry

    lax.fori_loop(0, rows // 32, body, 0)
    for out_at in (pl.ds(0, 8), pl.ds(rows + TOP, 8)):
        gather(out_at, 8, lambda ref, i, kind, f: (edge[kind, f, :, 0:128], edge[kind, f, :, 128:256]))


def ring_kernel(right, left, from_left, from_right, edge, ring, up, down):
    rows = right.shape[0]
    lanes = lane_of(rows)
    k = (lanes + 128 - HALO * GROUP) % 128 % GROUP
    mine = jnp.where(
        k <= 2,
        from_left[...],
        jnp.where(k <= 5, right[...], jnp.where(k <= 7, left[...], from_right[...])),
    )
    ring[0:rows, :] = mine
    flat = edge.reshape(edge.shape[0] * edge.shape[1] * 8, 256)
    for side in range(2):
        at = rows + side * flat.shape[0]
        ring[at : at + flat.shape[0], :] = flat[:, side * 128 : (side + 1) * 128]
    half = rows // 2
    for out, turn, turn_goal, frame, goal_frame in ((up, 80, 56, 1, 2), (down, 92, 80, 0, 0)):
        part = jnp.where(lanes < 36, pltpu.roll(mine, turn, 1), pltpu.roll(mine, turn_goal, 1))
        out[0:half, :] = jnp.where(lanes[0:half] < 64, part[0:half], pltpu.roll(part[half:], 64, 1))
        for side in range(2):
            cols = slice(side * 128, (side + 1) * 128)
            at = half + side * 40
            for n in range(5):
                tile = edge[0, frame + n, :, cols] if n < 3 else edge[1, goal_frame + n - 3, :, cols]
                out[at + 8 * n : at + 8 * n + 8, :] = tile


def sweep_kernel(
    ridge_part,
    slot_count,
    col_count,
    place,
    current,
    before,
    after,
    up,
    down,
    ring,
    ring_before,
    ring_after,
    video,
    multiplier,
    basis,
    coeff,
    shrunk_out,
    sent_out,
    s_a,
    s_b,
    goal,
    strip_a,
    strip_b,
    strip_goal,
    strip_flux,
    flux_f,
    flux_r,
    own_video,
    own_multiplier,
    own_basis,
    residual,
    out,
    sent,
    sums,
    sems,
):
    frames, rows, _ = current.shape
    all_rows = rows + 2 * TOP
    rank = basis.shape[0]
    row, col, slot = place[0], place[1], place[2]
    copies = []

    def copy(src, dst):
        c = pltpu.make_async_copy(src, dst, sems.at[len(copies)])
        c.start()
        copies.append(c)
        return c

    own_at = pl.ds(TOP, rows)
    strip_chunks = [(c, all_rows // 4) for c in range(0, all_rows, all_rows // 4)]
    first = []
    for half in range(2):
        at = pl.ds(half * 128, 128)
        for src, start, count, buf, at_frame in (
            (before, 0, HALO, s_a, 0),
            (current, 0, frames, s_a, HALO),
            (after, 0, HALO, s_a, HALO + frames),
            (before, HALO, 2, goal, 0),
            (down, HALO, 2, goal, 2),
            (up, HALO, 2, goal, 4),
            (after, HALO, 2, goal, 6),
        ):
            first.append(copy(src.at[pl.ds(start, count), :, at], buf.at[pl.ds(at_frame, count), half, own_at, :]))
    later = [copy(video, own_video), copy(multiplier, own_multiplier), copy(basis, own_basis)]

    folded = all_rows // 2
    for c, count in strip_chunks:
        at = slice(c, c + count)
        from_at = slice(c % folded, c % folded + count)
        lanes = lane_of(count)
        mine, prev, nxt = ring[at, :], ring_before[from_at, :], ring_after[from_at, :]
        turn = 64 if c >= folded else 0
        prev_own = pltpu.roll(prev, 64, 1) if turn else prev
        strip_a[at, :] = jnp.where(
            lanes < 36, prev_own, jnp.where(lanes < 84, mine, pltpu.roll(nxt, (84 + turn) % 128, 1))
        )
        strip_goal[at, :] = jnp.where(
            lanes < 36,
            pltpu.roll(prev, (104 + turn) % 128, 1),
            jnp.where(lanes < 84, pltpu.roll(mine, 80, 1), pltpu.roll(nxt, 48 + turn, 1)),
        )
    zero8 = jnp.zeros((8, 128), jnp.float32)
    for buf in (strip_a, strip_b):
        buf[pl.ds(all_rows, 8), :] = zero8
    for half in range(2):
        for g in range(2 * HALO + frames):
            goal_tile = None
            base = folded + half * 40
            if g < HALO:
                tile = ring_before[base + 8 * g : base + 8 * g + 8, :]
                if g >= 1:
                    goal_tile = ring_before[base + 8 * (g + 2) : base + 8 * (g + 2) + 8, :]
            elif g < HALO + frames:
                at = all_rows + half * 2 * frames * 8 + (g - HALO) * 8
                tile, goal_tile = ring[at : at + 8, :], ring[at + frames * 8 : at + frames * 8 + 8, :]
            else:
                n = g - HALO - frames
                tile = ring_after[base + 8 * n : base + 8 * n + 8, :]
                if n <= 1:
                    goal_tile = ring_after[base + 8 * (n + 3) : base + 8 * (n + 3) + 8, :]
            s_a[g, half, 0:TOP, :] = tile
            s_a[g, half, pl.ds(TOP + rows, 8), :] = tile
            s_a[g, half, pl.ds(all_rows, 8), :] = zero8
            s_b[g, half, pl.ds(all_rows, 8), :] = zero8
            if goal_tile is not None:
                goal[g - 1, half, 0:TOP, :] = goal_tile
                goal[g - 1, half, pl.ds(TOP + rows, 8), :] = goal_tile

    def first_row_last(value, count):
        return value[count - 1 : count, :]

    def down_one(value, carry, count):
        moved = pltpu.roll(value, 1, 0)
        return jnp.where(iota((count, 128), 0) == 0, jnp.broadcast_to(carry, (count, 128)), moved)

    def strip_sweep(old, new, flux_at):
        for c, count in strip_chunks:
            lanes = lane_of(count)
            k = lanes % GROUP
            s = old[c : c + count, :]
            s = jnp.where((slot == 0) & in_lanes(lanes, 24, 12), pltpu.roll(s, 116, 1), s)
            s = jnp.where((slot == slots_end) & in_lanes(lanes, 84, 12), pltpu.roll(s, 12, 1), s)
            s = jnp.where((col == 0) & (k == 2), pltpu.roll(s, 127, 1), s)
            s = jnp.where((col == cols_end) & (k == 8), pltpu.roll(s, 1, 1), s)
            old[c : c + count, :] = s

        @pl.when(row == 0)
        def _():
            old[TOP - 1 : TOP, :] = old[TOP : TOP + 1, :]

        @pl.when(row == 1)
        def _():
            old[TOP + rows : TOP + rows + 1, :] = old[TOP + rows - 1 : TOP + rows, :]

        carry = jnp.zeros((1, 128), jnp.float32)
        for c, count in strip_chunks:
            s = old[c : c + count, :]
            pf = pltpu.roll(s, 116, 1) - s
            pr = old[c + 1 : c + 1 + count, :] - s
            pc = pltpu.roll(s, 127, 1) - s
            weight = lax.rsqrt(FLOOR + pf * pf + pr * pr + pc * pc)
            ff, fr, fc = pf * weight, pr * weight, pc * weight
            k = lane_of(count) % GROUP
            strip_flux[flux_at, c : c + count, :] = jnp.where(k == 8, s, pltpu.roll(fc, 7, 1))
            spread = (
                (ff - pltpu.roll(ff, 12, 1)) + (fr - down_one(fr, carry, count)) + (fc - pltpu.roll(fc, 1, 1))
            )
            carry = first_row_last(fr, count)
            new[c : c + count, :] = s + RELAX * (strip_goal[c : c + count, :] - s + SMOOTH * spread)

    slots_end, cols_end = slot_count - 1, col_count - 1
    for half in range(2):
        flux_r[half, 0:8, :] = zero8
    strip_sweep(strip_a, strip_b, 0)

    for c in first:
        c.wait()

    chunks = [(c, min(64, all_rows - c)) for c in range(0, all_rows, 64)]

    def edges(old):
        @pl.when(slot == 0)
        def _():
            old[HALO - 1] = old[HALO]

        @pl.when(slot == slots_end)
        def _():
            old[HALO + frames] = old[HALO + frames - 1]

        @pl.when(row == 0)
        def _():
            for g in range(2 * HALO + frames):
                for half in range(2):
                    old[g, half, TOP - 1 : TOP, :] = old[g, half, TOP : TOP + 1, :]

        @pl.when(row == 1)
        def _():
            end = TOP + rows
            for g in range(2 * HALO + frames):
                for half in range(2):
                    old[g, half, end : end + 1, :] = old[g, half, end - 1 : end, :]

    last_keep = jnp.where((lane_of(8)[0:1] == 127) & (col == cols_end), 0.0, 1.0)

    def main_sweep(old, new, flux_at, g_first, g_count):
        edges(old)

        def body(i, carry0):
            g = g_first + i
            turn = (119 + 12 * 128 - 12 * g) % 128
            goal_at = jnp.maximum(g - 1, 0)
            for c, count in chunks:
                lanes = lane_of(count)
                at = pl.ds(c, count)
                next_at = pl.ds(c + 1, count)
                s = [old[g, half, at, :] for half in range(2)]
                turned = [pltpu.roll(x, 127, 1) for x in s]
                outside = pltpu.roll(strip_flux[flux_at, at, :], turn, 1)
                ahead = [
                    jnp.where(lanes == 127, turned[1], turned[0]),
                    jnp.where(lanes == 127, outside, turned[1]),
                ]
                fc, fr, ff = [], [], []
                for half in range(2):
                    x = s[half]
                    pf = old[g + 1, half, at, :] - x
                    pr = old[g, half, next_at, :] - x
                    pc = ahead[half] - x
                    if half == 1:
                        pc = pc * last_keep
                    weight = lax.rsqrt(FLOOR + pf * pf + pr * pr + pc * pc)
                    ff.append(pf * weight)
                    fr.append(pr * weight)
                    flux_r[half, pl.ds(c + 8, count), :] = fr[half]
                    fc.append(pc * weight)
                turned = [pltpu.roll(x, 1, 1) for x in fc]
                behind = [
                    jnp.where(lanes == 0, outside, turned[0]),
                    jnp.where(lanes == 0, turned[0], turned[1]),
                ]
                for half in range(2):
                    x = s[half]
                    spread = (
                        (ff[half] - flux_f[half, at, :])
                        + (fr[half] - flux_r[half, pl.ds(c + 7, count), :])
                        + (fc[half] - behind[half])
                    )
                    flux_f[half, at, :] = ff[half]
                    new[g, half, at, :] = x + RELAX * (goal[goal_at, half, at, :] - x + SMOOTH * spread)
            return carry0

        lax.fori_loop(0, g_count, body, 0)

    main_sweep(s_a, s_b, 0, 0, 9)
    strip_sweep(strip_b, strip_a, 1)
    main_sweep(s_b, s_a, 1, 1, 7)
    strip_sweep(strip_a, strip_b, 2)
    main_sweep(s_a, s_b, 2, 2, 5)

    for c in later:
        c.wait()
    sums[...] = jnp.zeros_like(sums)

    def finish(c, carry):
        chunk = 16
        at = pl.ds(pl.multiple_of(c * chunk, chunk), chunk)
        in_at = pl.ds(pl.multiple_of(c * chunk + TOP, 8), chunk)
        parts = []
        for f in range(frames):
            for half in range(2):
                cols = slice(half * 128, (half + 1) * 128)
                s = s_b[HALO + f, half, in_at, :]
                shrunk = s - jnp.clip(s, -shrink_level, shrink_level)
                out[f, at, cols] = shrunk
                r = own_video[f, at, cols] + dual_scale * own_multiplier[f, at, cols] - shrunk
                residual[half * frames + f, at, :] = r
                parts.append(r)
        for r in range(rank):
            images = [own_basis[r, at, half * 128 : (half + 1) * 128] for half in range(2)]
            for f in range(frames):
                term = images[0] * parts[2 * f] + images[1] * parts[2 * f + 1]
                sums[f * rank + r] += term[0:8] + term[8:16]
        return carry

    lax.fori_loop(0, rows // 16, finish, 0)
    done = copy(out, shrunk_out)
    lines = jnp.sum(sums[...], axis=1)
    total = lax.dot_general(
        jnp.ones((8, 128), jnp.float32),
        lines,
        (((1,), (1,)), ((), ())),
        precision=HIGHEST,
        preferred_element_type=jnp.float32,
    )
    cross = jnp.concatenate([total + ridge_part * coeff[...], jnp.zeros((8, 64), jnp.float32)], axis=1)
    chunk_rows = sent.shape[1]
    owned = rows // slot_count
    flat = sent.reshape(sent.shape[0] * chunk_rows, 128)

    def pack(j, carry):
        for f in range(frames):
            for half in range(2):
                flat[pl.ds(j * chunk_rows + half * frames + f, owned, stride=8), :] = residual[
                    half * frames + f, pl.ds(j * owned, owned), :
                ]
        sent[j, pl.ds(owned * 8, 8), :] = cross
        return carry

    done = [done]
    group = slot_count // 4
    for n in range(4):
        lax.fori_loop(n * group, (n + 1) * group, pack, 0)
        at = pl.ds(n * group, group)
        done.append(copy(sent.at[at], sent_out.at[at]))
    for c in done:
        c.wait()


def gram_kernel(slot, basis, out, old, sums, window):
    rank, rows, _ = basis.shape
    sums[...] = jnp.zeros_like(sums)

    def body(c, carry):
        at = pl.ds(pl.multiple_of(c * 8, 8), 8)
        images = [[basis[r, at, half * 128 : (half + 1) * 128] for half in range(2)] for r in range(rank)]
        for r in range(rank):
            for q in range(r, rank):
                sums[r * rank + q] += images[r][0] * images[q][0] + images[r][1] * images[q][1]
        return carry

    lax.fori_loop(0, rows // 8, body, 0)
    owned = old.shape[0]
    start = pl.multiple_of(slot[0] * owned // 8 * 8, 8)
    shift = slot[0] * owned - start
    flat = old.reshape(owned * 2 * rank, 128)
    for half in range(2):
        for r in range(rank):
            window[half * rank + r] = basis[r, pl.ds(start, 16), half * 128 : (half + 1) * 128]
            flat[pl.ds(half * rank + r, owned, stride=2 * rank), :] = window[half * rank + r, pl.ds(shift, owned), :]
    ones = jnp.ones((128, 128), jnp.float32)
    for r in range(rank):
        lines = jnp.concatenate(
            [jnp.sum(sums[min(r, q) * rank + max(r, q)], axis=0, keepdims=True) for q in range(rank)], axis=0
        )
        totals = dot(lines, ones)
        picked = jnp.where(iota((rank, 128), 0) == iota((rank, 128), 1), totals, 0.0)
        out[r : r + 1, :] = jnp.sum(picked, axis=0, keepdims=True)


def vmem(count):
    return [pl.BlockSpec(memory_space=pltpu.VMEM)] * count


def smem():
    return pl.BlockSpec(memory_space=pltpu.SMEM)


def anywhere(count):
    return [pl.BlockSpec(memory_space=pltpu.HBM)] * count


def floats(*shape):
    return jax.ShapeDtypeStruct(shape, jnp.float32)


LARGE = pltpu.CompilerParams(vmem_limit_bytes=28 * 1024 * 1024)
SMALL = pltpu.CompilerParams(vmem_limit_bytes=20 * 1024 * 1024)


def in_hbm(*shape):
    return pltpu.HBM(shape, jnp.float32)


def local(video, multiplier, foreground, basis, coefficients):
    plain = (video, multiplier)
    video, multiplier, basis = (pltpu.with_memory_space_constraint(x, pltpu.HBM) for x in (video, multiplier, basis))
    frames, rows, cols = video.shape
    rank = basis.shape[0]
    frame_count = lax.axis_size("frame")
    row_count = lax.axis_size("row")
    col_count = lax.axis_size("col")
    blocks = row_count * col_count
    frame_slot = lax.axis_index("frame")
    place = jnp.stack([lax.axis_index("row"), lax.axis_index("col"), frame_slot])
    all_rows = rows + 2 * TOP
    to_next = [(i, i + 1) for i in range(frame_count - 1)]
    to_previous = [(b, a) for a, b in to_next]
    to_right = [(i, i + 1) for i in range(col_count - 1)]
    to_left = [(b, a) for a, b in to_right]

    edge = pl.pallas_call(
        edge_kernel,
        out_shape=floats(2, frames, 8, cols),
        in_specs=[smem(), smem()] + anywhere(4),
        out_specs=vmem(1)[0],
        scratch_shapes=[pltpu.VMEM((n, 8, cols), jnp.float32) for n in (frames, frames, rank, frames)]
        + [pltpu.SemaphoreType.DMA((4,))],
        name="edge",
    )(place, coefficients, video, multiplier, basis, foreground)
    edge = lax.ppermute(edge, "row", [(0, 1), (1, 0)])
    up, down = pl.pallas_call(
        target_kernel,
        out_shape=(pltpu.VMEM((HALO + 2, rows, cols), jnp.float32), pltpu.VMEM((HALO + 2, rows, cols), jnp.float32)),
        in_specs=[smem()] + vmem(2) + anywhere(1) + vmem(1),
        out_specs=vmem(2),
        scratch_shapes=[pltpu.VMEM(basis.shape, jnp.float32), pltpu.SemaphoreType.DMA((6,))],
        compiler_params=SMALL,
        name="target",
    )(coefficients, *plain, basis, foreground)
    up, down, edge = lax.optimization_barrier((up, down, edge))
    before = lax.ppermute(up, "frame", to_next)
    after = lax.ppermute(down, "frame", to_previous)
    right, left = pl.pallas_call(
        strips_kernel,
        out_shape=(floats(all_rows, 128), floats(all_rows, 128)),
        in_specs=vmem(4),
        out_specs=vmem(2),
        compiler_params=SMALL,
        name="strips",
    )(foreground, up, down, edge)
    from_left = lax.ppermute(right, "col", to_right)
    from_right = lax.ppermute(left, "col", to_left)
    folded = all_rows // 2
    ring, ring_up, ring_down = pl.pallas_call(
        ring_kernel,
        out_shape=(floats(all_rows + 16 * frames * 2, 128), floats(folded + 80, 128), floats(folded + 80, 128)),
        in_specs=vmem(5),
        out_specs=vmem(3),
        compiler_params=SMALL,
        name="ring",
    )(right, left, from_left, from_right, edge)
    ring_before = lax.ppermute(ring_up, "frame", to_next)
    ring_after = lax.ppermute(ring_down, "frame", to_previous)

    pixel_ridge = ridge_share * rows * cols * blocks
    owned_rows = rows // frame_count
    main = (2 * HALO + frames, 2, all_rows + 8, 128)
    strip = (all_rows + 8, 128)
    scratch = [
        main,
        main,
        (2 * HALO + frames - 2, 2, all_rows, 128),
        strip,
        strip,
        (all_rows, 128),
        (3, all_rows, 128),
        (2, all_rows, 128),
        (2, all_rows + 8, 128),
        video.shape,
        video.shape,
        basis.shape,
        (2 * frames, rows, 128),
        video.shape,
        (frame_count, owned_rows * 8 + 8, 128),
        (frames * rank, 8, 128),
    ]
    shrunk, sent = pl.pallas_call(
        functools.partial(sweep_kernel, pixel_ridge / blocks, frame_count, col_count),
        out_shape=(in_hbm(frames, rows, cols), in_hbm(frame_count, owned_rows * 8 + 8, 128)),
        in_specs=[smem()] + anywhere(5) + vmem(3) + anywhere(3) + vmem(1),
        out_specs=anywhere(2),
        scratch_shapes=[pltpu.VMEM(s, jnp.float32) for s in scratch] + [pltpu.SemaphoreType.DMA((22,))],
        compiler_params=LARGE,
        name="sweeps",
    )(
        place,
        foreground,
        before,
        after,
        up,
        down,
        ring,
        ring_before,
        ring_after,
        video,
        multiplier,
        basis,
        coefficients.reshape(1, frames * rank),
    )
    got = lax.all_to_all(sent, "frame", 0, 0, tiled=True)
    basis, _ = lax.optimization_barrier((basis, sent))
    gram, old_owned = pl.pallas_call(
        gram_kernel,
        out_shape=(floats(rank, 128), floats(owned_rows, 2 * rank, 128)),
        in_specs=[smem()] + vmem(1),
        out_specs=vmem(2),
        scratch_shapes=[
            pltpu.VMEM((rank * rank, 8, 128), jnp.float32),
            pltpu.VMEM((2 * rank, 16, 128), jnp.float32),
        ],
        compiler_params=SMALL,
        name="gram",
    )(frame_slot.reshape(1), basis)
    parts = jnp.concatenate([got[:, owned_rows * 8, :], gram], axis=0)
    parts = lax.all_to_all(jnp.broadcast_to(parts[None], (blocks, *parts.shape)), ("row", "col"), 0, 0, tiled=True)
    frame_ridge = ridge_share * frames * frame_count
    new_basis, new_coeff = pl.pallas_call(
        functools.partial(final_kernel, pixel_ridge, frame_ridge),
        out_shape=(floats(owned_rows, rank, cols), floats(frames, rank)),
        in_specs=[smem()] + vmem(3),
        out_specs=vmem(2),
        scratch_shapes=[pltpu.VMEM((frame_count, 128), jnp.float32)],
        compiler_params=SMALL,
        name="final",
    )(frame_slot.reshape(1), got, parts, old_owned)
    return shrunk, new_coeff, new_basis.transpose(1, 0, 2)


def solution(mesh):
    placed = (
        P("frame", "row", "col"),
        P("frame", "row", "col"),
        P("frame", "row", "col"),
        P(None, "row", "col"),
        P("frame", None),
    )
    return jax.shard_map(
        local,
        mesh=mesh,
        in_specs=placed,
        out_specs=(P("frame", "row", "col"), P("frame", None), P(None, ("row", "frame"), "col")),
        check_vma=False,
    )
```

```python
import functools

import jax
import jax.numpy as jnp
from jax import lax
from jax.experimental import pallas as pl
from jax.experimental.pallas import tpu as pltpu
from jax.sharding import PartitionSpec as P

PASSES = 3


relax_rate = 0.8
smooth_weight = 0.5
smooth_floor = 0.25
shrink_level = 0.4
dual_scale = 0.8
ridge_share = 0.1


HIGHEST = lax.Precision.HIGHEST


def iota(shape, dim):
    return lax.broadcasted_iota(jnp.int32, shape, dim)


def dot(a, b):
    return jnp.dot(a, b, precision=HIGHEST, preferred_element_type=jnp.float32)


def eliminated(matrix):
    n = matrix.shape[0]
    wide = (n, 128)
    lanes, rows = iota(wide, 1), iota(wide, 0)
    work = jnp.concatenate([matrix, jnp.zeros((n, 128 - n), jnp.float32)], axis=1)
    work = work + jnp.where(lanes == rows + n, 1.0, 0.0)
    for k in range(0, n, 2):
        col0 = jnp.broadcast_to(work[:, k : k + 1], wide)
        col1 = jnp.broadcast_to(work[:, k + 1 : k + 2], wide)
        row0, row1 = work[k : k + 1, :], work[k + 1 : k + 2, :]
        a, b, d = col0[k : k + 1, :], col1[k : k + 1, :], col1[k + 1 : k + 2, :]
        scale = 1.0 / (a * d - b * b)
        new0 = jnp.broadcast_to((d * row0 - b * row1) * scale, wide)
        new1 = jnp.broadcast_to((a * row1 - b * row0) * scale, wide)
        left = work - col0 * new0 - col1 * new1
        work = jnp.where(rows == k, new0, jnp.where(rows == k + 1, new1, left))
    return work[:, n : 2 * n]


def spread_ranks(rank, width):
    return jnp.where(iota((width, rank), 0) % rank == iota((width, rank), 1), 1.0, 0.0)


def spread_blocks(block, width, count):
    rank = block.shape[0]
    pick = spread_ranks(rank, width)
    full = dot(dot(pick, block), pick.T)
    a, b = iota((width, width), 0) // rank, iota((width, width), 1) // rank
    return jnp.where((a == b) & (a < count), full, 0.0)


def final_kernel(pixel_ridge, ridge, got_ref, parts_ref, old_ref, basis_ref, coeff_ref, coeff_all):
    step = 8 * basis_ref.shape[0] + 1
    slots = got_ref.shape[0] // step
    rank = basis_ref.shape[1]
    rows_owned = basis_ref.shape[0]
    total = parts_ref[0]
    for peer in range(1, parts_ref.shape[0]):
        total = total + parts_ref[peer]
    eye = jnp.where(iota((rank, rank), 0) == iota((rank, rank), 1), 1.0, 0.0)
    inverse = eliminated(total[slots:, 0:rank] + pixel_ridge * eye)
    coeff = dot(total[0:slots], spread_blocks(inverse, 128, 4))
    coeff_all[0:slots] = coeff
    mine = coeff_all[pl.ds(lax.axis_index("frame"), 1), :]
    for f in range(4):
        coeff_ref[f : f + 1, :] = mine[:, f * rank : (f + 1) * rank]
    width = 128
    coeff_t = coeff.T
    full = dot(coeff_t, coeff)
    a, b = iota((width, width), 0) // rank, iota((width, width), 1) // rank
    pick = spread_ranks(rank, width)
    gram = dot(dot(pick.T, jnp.where(a == b, full, 0.0)), pick)
    lines = 8 * slots
    repeat = jnp.where(iota((slots, lines), 0) == iota((slots, lines), 1) // 8, 1.0, 0.0)
    wide = dot(coeff_t, repeat)
    wide = jnp.where(iota((width, lines), 0) // rank == iota((width, lines), 1) % 4, wide, 0.0)
    narrow = wide[0:rank]
    for f in range(1, 4):
        narrow = narrow + wide[f * rank : (f + 1) * rank]
    twice = jnp.concatenate([narrow, narrow], axis=0)
    factor = jnp.where(
        iota((2 * rank, lines), 0) // rank == (iota((2 * rank, lines), 1) // 4) % 2, twice, 0.0
    )
    sums = []
    for i in range(0, rows_owned):
        block = jnp.concatenate(
            [got_ref[n * step + 8 * i : n * step + 8 * (i + 1), :] for n in range(slots)], axis=0
        )
        sums.append(dot(factor, block) + ridge * old_ref[i])
    inverse = spread_blocks(eliminated(gram + ridge * eye), 2 * rank, 2)
    for i in range(rows_owned):
        rows = dot(inverse, sums[i])
        for half in range(2):
            basis_ref[i, :, half * 128 : (half + 1) * 128] = rows[half * rank : (half + 1) * rank]


HALO = 3
GROUP = 12
TOP = 8
FLOOR, SMOOTH, RELAX = smooth_floor, smooth_weight, relax_rate


def lane_of(rows):
    return iota((rows, 128), 1)


def in_lanes(lanes, first, count):
    first = first % 128
    if first + count <= 128:
        return (lanes >= first) & (lanes < first + count)
    return (lanes >= first) | (lanes < first + count - 128)


def goal_rows(coeff, video, multiplier, basis, at, which=range(4)):
    sums = [None] * len(which)
    for r in range(basis.shape[0]):
        image = basis[r, at, :]
        for k, f in enumerate(which):
            term = coeff[f, r] * image
            sums[k] = term if r == 0 else sums[k] + term
    return [video[f, at, :] - sums[k] + dual_scale * multiplier[f, at, :] for k, f in enumerate(which)]


def edge_kernel(coeff, video, multiplier, basis, current, edge, *scratch):
    buffers, sems = scratch[:-1], scratch[-1]
    frames, rows, _ = video.shape
    at = pl.ds(pl.multiple_of((1 - lax.axis_index("row")) * (rows - 8), 8), 8)
    near = [
        pltpu.make_async_copy(ref.at[:, at, :], buf, sems.at[k])
        for k, (ref, buf) in enumerate(zip((video, multiplier, basis, current), buffers))
    ]
    for c in near:
        c.start()
    for c in near:
        c.wait()
    video, multiplier, basis, current = buffers
    edge[0] = current[...]
    for f, value in enumerate(goal_rows(coeff, video, multiplier, basis, slice(0, 8))):
        edge[1, f] = value


def fill_side(forward, coeff, video, multiplier, basis, current, out, ready):
    frames, rows, _ = video.shape
    chunk, piece = 24, rows // len(ready)
    for k in range(HALO):
        out[k] = current[frames - HALO + k if forward else k]
    goals = (frames - 2, frames - 1) if forward else (0, 1)
    for p, wait in enumerate(ready):
        wait()

        def body(c, carry):
            at = pl.ds(pl.multiple_of(p * piece + c * chunk, 8), chunk)
            for k, value in enumerate(goal_rows(coeff, video, multiplier, basis, at, goals)):
                out[HALO + k, at, :] = value
            return carry

        lax.fori_loop(0, piece // chunk, body, 0)


def first_side_kernel(coeff, video, multiplier, basis_in, current, out, basis, sems):
    pieces = sems.shape[0]
    piece = basis.shape[1] // pieces
    copies = []
    for p in range(pieces):
        at = pl.ds(p * piece, piece)
        copies.append(pltpu.make_async_copy(basis_in.at[:, at, :], basis.at[:, at, :], sems.at[p]))
        copies[p].start()
    fill_side(False, coeff, video, multiplier, basis, current, out, [c.wait for c in copies])


def second_side_kernel(coeff, video, multiplier, basis, current, out):
    fill_side(True, coeff, video, multiplier, basis, current, out, [lambda: None])


def strips_kernel(up, down, edge, right, left):
    frames, rows = edge.shape[1], up.shape[1]
    sources = [(up if f > 0 else down, max(f - 1, 0), HALO * GROUP + GROUP * f, 0, f) for f in range(frames)]
    sources += [
        (down if f < 2 else up, HALO + f % 2, HALO * GROUP + GROUP * (f + frames), 1, f) for f in range(frames)
    ]

    def gather(out_at, count, pick):
        lanes = lane_of(count)
        a = jnp.zeros((count, 128), jnp.float32)
        b = a
        for ref, index, base, kind, f in sources:
            first, last = pick(ref, index, kind, f)
            both = jnp.where(lanes < 64, first, last)
            here = in_lanes(lanes, base, GROUP)
            a = jnp.where(here, pltpu.roll(both, (base + 3) % 128, 1), a)
            b = jnp.where(here, pltpu.roll(both, (base + 8) % 128, 1), b)
        right[out_at, :] = a
        left[out_at, :] = b

    def body(c, carry):
        at = pl.ds(pl.multiple_of(c * 32, 32), 32)
        out_at = pl.ds(pl.multiple_of(c * 32 + TOP, 8), 32)
        gather(out_at, 32, lambda ref, i, kind, f: (ref[i, at, 0:128], ref[i, at, 128:256]))
        return carry

    lax.fori_loop(0, rows // 32, body, 0)
    for out_at in (pl.ds(0, 8), pl.ds(rows + TOP, 8)):
        gather(out_at, 8, lambda ref, i, kind, f: (edge[kind, f, :, 0:128], edge[kind, f, :, 128:256]))


def ring_kernel(right, left, from_left, from_right, edge, ring, up, down):
    rows = right.shape[0]
    lanes = lane_of(rows)
    k = (lanes + 128 - HALO * GROUP) % 128 % GROUP
    mine = jnp.where(
        k <= 2,
        from_left[...],
        jnp.where(k <= 5, right[...], jnp.where(k <= 7, left[...], from_right[...])),
    )
    ring[0:rows, :] = mine
    flat = edge.reshape(edge.shape[0] * edge.shape[1] * 8, 256)
    for side in range(2):
        at = rows + side * flat.shape[0]
        ring[at : at + flat.shape[0], :] = flat[:, side * 128 : (side + 1) * 128]
    half = rows // 2
    for out, turn, turn_goal, frame, goal_frame in ((up, 80, 56, 1, 2), (down, 92, 80, 0, 0)):
        part = jnp.where(lanes < 36, pltpu.roll(mine, turn, 1), pltpu.roll(mine, turn_goal, 1))
        out[0:half, :] = jnp.where(lanes[0:half] < 64, part[0:half], pltpu.roll(part[half:], 64, 1))
        for side in range(2):
            cols = slice(side * 128, (side + 1) * 128)
            at = half + side * 40
            for n in range(5):
                tile = edge[0, frame + n, :, cols] if n < 3 else edge[1, goal_frame + n - 3, :, cols]
                out[at + 8 * n : at + 8 * n + 8, :] = tile


def sweep_kernel(
    ridge_part,
    slot_count,
    col_count,
    current,
    before,
    after,
    up,
    down,
    ring,
    ring_before,
    ring_after,
    video,
    multiplier,
    basis,
    coeff,
    shrunk_out,
    sent_out,
    s_a,
    s_b,
    goal,
    strip_a,
    strip_b,
    strip_goal,
    strip_flux,
    flux_f,
    flux_r,
    own_video,
    own_multiplier,
    own_basis,
    residual,
    out,
    sent,
    sums,
    sems,
):
    frames, rows, _ = current.shape
    all_rows = rows + 2 * TOP
    rank = basis.shape[0]
    row, col, slot = lax.axis_index("row"), lax.axis_index("col"), lax.axis_index("frame")
    copies = []

    def copy(src, dst):
        c = pltpu.make_async_copy(src, dst, sems.at[len(copies)])
        c.start()
        copies.append(c)
        return c

    own_at = pl.ds(TOP, rows)
    strip_chunks = [(0, 80), (80, all_rows // 2 - 80)]
    strip_chunks += [(all_rows // 2 + c, count) for c, count in strip_chunks]
    first = []
    for half in range(2):
        at = pl.ds(half * 128, 128)
        for src, start, count, buf, at_frame in (
            (before, 0, HALO, s_a, 0),
            (current, 0, frames, s_a, HALO),
            (after, 0, HALO, s_a, HALO + frames),
            (before, HALO, 2, goal, 0),
            (down, HALO, 2, goal, 2),
            (up, HALO, 2, goal, 4),
            (after, HALO, 2, goal, 6),
        ):
            first.append(copy(src.at[pl.ds(start, count), :, at], buf.at[pl.ds(at_frame, count), half, own_at, :]))
    later = [copy(video, own_video), copy(multiplier, own_multiplier), copy(basis, own_basis)]

    folded = all_rows // 2
    for c, count in strip_chunks:
        at = slice(c, c + count)
        from_at = slice(c % folded, c % folded + count)
        lanes = lane_of(count)
        mine, prev, nxt = ring[at, :], ring_before[from_at, :], ring_after[from_at, :]
        turn = 64 if c >= folded else 0
        prev_own = pltpu.roll(prev, 64, 1) if turn else prev
        strip_a[at, :] = jnp.where(
            lanes < 36, prev_own, jnp.where(lanes < 84, mine, pltpu.roll(nxt, (84 + turn) % 128, 1))
        )
        strip_goal[at, :] = jnp.where(
            lanes < 36,
            pltpu.roll(prev, (104 + turn) % 128, 1),
            jnp.where(lanes < 84, pltpu.roll(mine, 80, 1), pltpu.roll(nxt, 48 + turn, 1)),
        )
    zero8 = jnp.zeros((8, 128), jnp.float32)
    for buf in (strip_a, strip_b):
        buf[pl.ds(all_rows, 8), :] = zero8
    for half in range(2):
        for g in range(2 * HALO + frames):
            goal_tile = None
            base = folded + half * 40
            if g < HALO:
                tile = ring_before[base + 8 * g : base + 8 * g + 8, :]
                if g >= 1:
                    goal_tile = ring_before[base + 8 * (g + 2) : base + 8 * (g + 2) + 8, :]
            elif g < HALO + frames:
                at = all_rows + half * 2 * frames * 8 + (g - HALO) * 8
                tile, goal_tile = ring[at : at + 8, :], ring[at + frames * 8 : at + frames * 8 + 8, :]
            else:
                n = g - HALO - frames
                tile = ring_after[base + 8 * n : base + 8 * n + 8, :]
                if n <= 1:
                    goal_tile = ring_after[base + 8 * (n + 3) : base + 8 * (n + 3) + 8, :]
            s_a[g, half, 0:TOP, :] = tile
            s_a[g, half, pl.ds(TOP + rows, 8), :] = tile
            s_a[g, half, pl.ds(all_rows, 8), :] = zero8
            s_b[g, half, pl.ds(all_rows, 8), :] = zero8
            if goal_tile is not None:
                goal[g - 1, half, 0:TOP, :] = goal_tile
                goal[g - 1, half, pl.ds(TOP + rows, 8), :] = goal_tile

    def first_row_last(value, count):
        return value[count - 1 : count, :]

    def down_one(value, carry, count):
        moved = pltpu.roll(value, 1, 0)
        return jnp.where(iota((count, 128), 0) == 0, jnp.broadcast_to(carry, (count, 128)), moved)

    def strip_sweep(old, new, flux_at):
        for c, count in strip_chunks:
            lanes = lane_of(count)
            k = lanes % GROUP
            s = old[c : c + count, :]
            s = jnp.where((slot == 0) & in_lanes(lanes, 24, 12), pltpu.roll(s, 116, 1), s)
            s = jnp.where((slot == slots_end) & in_lanes(lanes, 84, 12), pltpu.roll(s, 12, 1), s)
            s = jnp.where((col == 0) & (k == 2), pltpu.roll(s, 127, 1), s)
            s = jnp.where((col == cols_end) & (k == 8), pltpu.roll(s, 1, 1), s)
            old[c : c + count, :] = s

        @pl.when(row == 0)
        def _():
            old[TOP - 1 : TOP, :] = old[TOP : TOP + 1, :]

        @pl.when(row == 1)
        def _():
            old[TOP + rows : TOP + rows + 1, :] = old[TOP + rows - 1 : TOP + rows, :]

        carry = jnp.zeros((1, 128), jnp.float32)
        for c, count in strip_chunks:
            s = old[c : c + count, :]
            pf = pltpu.roll(s, 116, 1) - s
            pr = old[c + 1 : c + 1 + count, :] - s
            pc = pltpu.roll(s, 127, 1) - s
            weight = lax.rsqrt(FLOOR + pf * pf + pr * pr + pc * pc)
            ff, fr, fc = pf * weight, pr * weight, pc * weight
            k = lane_of(count) % GROUP
            strip_flux[flux_at, c : c + count, :] = jnp.where(k == 8, s, pltpu.roll(fc, 7, 1))
            spread = (
                (ff - pltpu.roll(ff, 12, 1)) + (fr - down_one(fr, carry, count)) + (fc - pltpu.roll(fc, 1, 1))
            )
            carry = first_row_last(fr, count)
            new[c : c + count, :] = s + RELAX * (strip_goal[c : c + count, :] - s + SMOOTH * spread)

    slots_end, cols_end = slot_count - 1, col_count - 1
    for half in range(2):
        flux_r[half, 0:8, :] = zero8
    strip_sweep(strip_a, strip_b, 0)

    for c in first:
        c.wait()

    chunks = [(c, min(64, all_rows - c)) for c in range(0, all_rows, 64)]

    def edges(old):
        @pl.when(slot == 0)
        def _():
            old[HALO - 1] = old[HALO]

        @pl.when(slot == slots_end)
        def _():
            old[HALO + frames] = old[HALO + frames - 1]

        @pl.when(row == 0)
        def _():
            for g in range(2 * HALO + frames):
                for half in range(2):
                    old[g, half, TOP - 1 : TOP, :] = old[g, half, TOP : TOP + 1, :]

        @pl.when(row == 1)
        def _():
            end = TOP + rows
            for g in range(2 * HALO + frames):
                for half in range(2):
                    old[g, half, end : end + 1, :] = old[g, half, end - 1 : end, :]

    last_keep = jnp.where((lane_of(8)[0:1] == 127) & (col == cols_end), 0.0, 1.0)

    def main_sweep(old, new, flux_at, g_first, g_count):
        edges(old)

        def body(i, carry0):
            g = g_first + i
            turn = (119 + 12 * 128 - 12 * g) % 128
            goal_at = jnp.maximum(g - 1, 0)
            for c, count in chunks:
                lanes = lane_of(count)
                at = pl.ds(c, count)
                next_at = pl.ds(c + 1, count)
                s = [old[g, half, at, :] for half in range(2)]
                turned = [pltpu.roll(x, 127, 1) for x in s]
                outside = pltpu.roll(strip_flux[flux_at, at, :], turn, 1)
                ahead = [
                    jnp.where(lanes == 127, turned[1], turned[0]),
                    jnp.where(lanes == 127, outside, turned[1]),
                ]
                fc, fr, ff = [], [], []
                for half in range(2):
                    x = s[half]
                    pf = old[g + 1, half, at, :] - x
                    pr = old[g, half, next_at, :] - x
                    pc = ahead[half] - x
                    if half == 1:
                        pc = pc * last_keep
                    weight = lax.rsqrt(FLOOR + pf * pf + pr * pr + pc * pc)
                    ff.append(pf * weight)
                    fr.append(pr * weight)
                    flux_r[half, pl.ds(c + 8, count), :] = fr[half]
                    fc.append(pc * weight)
                turned = [pltpu.roll(x, 1, 1) for x in fc]
                behind = [
                    jnp.where(lanes == 0, outside, turned[0]),
                    jnp.where(lanes == 0, turned[0], turned[1]),
                ]
                for half in range(2):
                    x = s[half]
                    spread = (
                        (ff[half] - flux_f[half, at, :])
                        + (fr[half] - flux_r[half, pl.ds(c + 7, count), :])
                        + (fc[half] - behind[half])
                    )
                    flux_f[half, at, :] = ff[half]
                    new[g, half, at, :] = x + RELAX * (goal[goal_at, half, at, :] - x + SMOOTH * spread)
            return carry0

        lax.fori_loop(0, g_count, body, 0)

    main_sweep(s_a, s_b, 0, 0, 9)
    strip_sweep(strip_b, strip_a, 1)
    main_sweep(s_b, s_a, 1, 1, 7)
    strip_sweep(strip_a, strip_b, 2)
    main_sweep(s_a, s_b, 2, 2, 5)

    for c in later:
        c.wait()
    sums[...] = jnp.zeros_like(sums)

    def finish(c, carry):
        chunk = 16
        at = pl.ds(pl.multiple_of(c * chunk, chunk), chunk)
        in_at = pl.ds(pl.multiple_of(c * chunk + TOP, 8), chunk)
        parts = []
        for f in range(frames):
            for half in range(2):
                cols = slice(half * 128, (half + 1) * 128)
                s = s_b[HALO + f, half, in_at, :]
                shrunk = s - jnp.clip(s, -shrink_level, shrink_level)
                out[f, at, cols] = shrunk
                r = own_video[f, at, cols] + dual_scale * own_multiplier[f, at, cols] - shrunk
                residual[half * frames + f, at, :] = r
                parts.append(r)
        for r in range(rank):
            images = [own_basis[r, at, half * 128 : (half + 1) * 128] for half in range(2)]
            for f in range(frames):
                term = images[0] * parts[2 * f] + images[1] * parts[2 * f + 1]
                sums[f * rank + r] += term[0:8] + term[8:16]
        return carry

    lax.fori_loop(0, rows // 16, finish, 0)
    done = copy(out, shrunk_out)
    lines = jnp.sum(sums[...], axis=1)
    total = lax.dot_general(
        jnp.ones((8, 128), jnp.float32),
        lines,
        (((1,), (1,)), ((), ())),
        precision=HIGHEST,
        preferred_element_type=jnp.float32,
    )
    cross = jnp.concatenate([total[0:1] + ridge_part * coeff[...], jnp.zeros((1, 64), jnp.float32)], axis=1)
    owned = rows // slot_count
    chunk_rows = owned * 8 + 1

    def pack(j, carry):
        for f in range(frames):
            for half in range(2):
                sent[pl.ds(j * chunk_rows + half * frames + f, owned, stride=8), :] = residual[
                    half * frames + f, pl.ds(j * owned, owned), :
                ]
        sent[pl.ds(j * chunk_rows + owned * 8, 1), :] = cross
        return carry

    done = [done]
    group = slot_count // 4
    for n in range(4):
        lax.fori_loop(n * group, (n + 1) * group, pack, 0)
        at = pl.ds(n * group * chunk_rows, group * chunk_rows)
        done.append(copy(sent.at[at], sent_out.at[at]))
    for c in done:
        c.wait()


def gram_kernel(slot_count, basis, out, old, sums, window):
    rank, rows, _ = basis.shape
    sums[...] = jnp.zeros_like(sums)

    def body(c, carry):
        at = pl.ds(pl.multiple_of(c * 8, 8), 8)
        images = [[basis[r, at, half * 128 : (half + 1) * 128] for half in range(2)] for r in range(rank)]
        for r in range(rank):
            for q in range(r, rank):
                sums[r * rank + q] += images[r][0] * images[q][0] + images[r][1] * images[q][1]
        return carry

    lax.fori_loop(0, rows // 8, body, 0)
    owned = rows // slot_count
    start = pl.multiple_of(lax.axis_index("frame") * owned // 8 * 8, 8)
    shift = lax.axis_index("frame") * owned - start
    flat = old.reshape(old.shape[0] * 2 * rank, 128)
    for half in range(2):
        for r in range(rank):
            window[half * rank + r, 0:16] = basis[r, pl.ds(start, 16), half * 128 : (half + 1) * 128]
            flat[pl.ds(half * rank + r, owned, stride=2 * rank), :] = window[half * rank + r, pl.ds(shift, owned), :]
    ones = jnp.ones((128, 128), jnp.float32)
    for r in range(rank):
        lines = jnp.concatenate(
            [jnp.sum(sums[min(r, q) * rank + max(r, q)], axis=0, keepdims=True) for q in range(rank)], axis=0
        )
        totals = dot(lines, ones)
        picked = jnp.where(iota((rank, 128), 0) == iota((rank, 128), 1), totals, 0.0)
        out[r : r + 1, :] = jnp.sum(picked, axis=0, keepdims=True)


def vmem(count):
    return [pl.BlockSpec(memory_space=pltpu.VMEM)] * count


def smem():
    return pl.BlockSpec(memory_space=pltpu.SMEM)


def anywhere(count):
    return [pl.BlockSpec(memory_space=pltpu.HBM)] * count


def floats(*shape):
    return jax.ShapeDtypeStruct(shape, jnp.float32)


LARGE = pltpu.CompilerParams(vmem_limit_bytes=28 * 1024 * 1024)
SMALL = pltpu.CompilerParams(vmem_limit_bytes=20 * 1024 * 1024)


def in_hbm(*shape):
    return pltpu.HBM(shape, jnp.float32)


def local(video, multiplier, foreground, basis, coefficients):
    plain = (video, multiplier)
    video, multiplier, basis = (pltpu.with_memory_space_constraint(x, pltpu.HBM) for x in (video, multiplier, basis))
    frames, rows, cols = video.shape
    rank = basis.shape[0]
    frame_count = lax.axis_size("frame")
    row_count = lax.axis_size("row")
    col_count = lax.axis_size("col")
    blocks = row_count * col_count
    all_rows = rows + 2 * TOP
    to_next = [(i, i + 1) for i in range(frame_count - 1)]
    to_previous = [(b, a) for a, b in to_next]
    to_right = [(i, i + 1) for i in range(col_count - 1)]
    to_left = [(b, a) for a, b in to_right]

    edge = pl.pallas_call(
        edge_kernel,
        out_shape=floats(2, frames, 8, cols),
        in_specs=[smem()] + anywhere(4),
        out_specs=vmem(1)[0],
        scratch_shapes=[pltpu.VMEM((n, 8, cols), jnp.float32) for n in (frames, frames, rank, frames)]
        + [pltpu.SemaphoreType.DMA((4,))],
        name="edge",
    )(coefficients, video, multiplier, basis, foreground)
    edge = lax.ppermute(edge, "row", [(0, 1), (1, 0)])
    down, images = pl.pallas_call(
        first_side_kernel,
        out_shape=(pltpu.VMEM((HALO + 2, rows, cols), jnp.float32), pltpu.VMEM(basis.shape, jnp.float32)),
        in_specs=[smem()] + vmem(2) + anywhere(1) + vmem(1),
        out_specs=vmem(2),
        scratch_shapes=[pltpu.SemaphoreType.DMA((6,))],
        compiler_params=SMALL,
        name="first_side",
    )(coefficients, *plain, basis, foreground)
    up = pl.pallas_call(
        second_side_kernel,
        out_shape=pltpu.VMEM((HALO + 2, rows, cols), jnp.float32),
        in_specs=[smem()] + vmem(4),
        out_specs=vmem(1)[0],
        compiler_params=SMALL,
        name="second_side",
    )(coefficients, *plain, images, foreground)
    up, edge = lax.optimization_barrier((up, edge))
    before = lax.ppermute(up, "frame", to_next)
    after = lax.ppermute(down, "frame", to_previous)
    right, left = pl.pallas_call(
        strips_kernel,
        out_shape=(floats(all_rows, 128), floats(all_rows, 128)),
        in_specs=vmem(3),
        out_specs=vmem(2),
        compiler_params=SMALL,
        name="strips",
    )(up, down, edge)
    from_left = lax.ppermute(right, "col", to_right)
    from_right = lax.ppermute(left, "col", to_left)
    folded = all_rows // 2
    ring, ring_up, ring_down = pl.pallas_call(
        ring_kernel,
        out_shape=(floats(all_rows + 16 * frames * 2, 128), floats(folded + 80, 128), floats(folded + 80, 128)),
        in_specs=vmem(5),
        out_specs=vmem(3),
        compiler_params=SMALL,
        name="ring",
    )(right, left, from_left, from_right, edge)
    ring_before = lax.ppermute(ring_up, "frame", to_next)
    ring_after = lax.ppermute(ring_down, "frame", to_previous)

    pixel_ridge = ridge_share * rows * cols * blocks
    owned_rows = rows // frame_count
    main = (2 * HALO + frames, 2, all_rows + 8, 128)
    strip = (all_rows + 8, 128)
    scratch = [
        main,
        main,
        (2 * HALO + frames - 2, 2, all_rows, 128),
        strip,
        strip,
        (all_rows, 128),
        (3, all_rows, 128),
        (2, all_rows, 128),
        (2, all_rows + 8, 128),
        video.shape,
        video.shape,
        basis.shape,
        (2 * frames, rows + 16, 128),
        video.shape,
        (frame_count * (owned_rows * 8 + 1) + 64, 128),
        (frames * rank, 8, 128),
    ]
    shrunk, sent = pl.pallas_call(
        functools.partial(sweep_kernel, pixel_ridge / blocks, frame_count, col_count),
        out_shape=(in_hbm(frames, rows, cols), in_hbm(frame_count * (owned_rows * 8 + 1), 128)),
        in_specs=anywhere(5) + vmem(3) + anywhere(3) + vmem(1),
        out_specs=anywhere(2),
        scratch_shapes=[pltpu.VMEM(s, jnp.float32) for s in scratch] + [pltpu.SemaphoreType.DMA((22,))],
        compiler_params=LARGE,
        name="sweeps",
    )(
        foreground,
        before,
        after,
        up,
        down,
        ring,
        ring_before,
        ring_after,
        video,
        multiplier,
        basis,
        coefficients.reshape(1, frames * rank),
    )
    got = lax.all_to_all(sent.reshape(frame_count, owned_rows * 8 + 1, 1, 128), "frame", 0, 0, tiled=True)
    basis, _ = lax.optimization_barrier((basis, sent))
    gram, old_owned = pl.pallas_call(
        functools.partial(gram_kernel, frame_count),
        out_shape=(floats(rank, 128), floats(16, 2 * rank, 128)),
        in_specs=vmem(1),
        out_specs=vmem(2),
        scratch_shapes=[
            pltpu.VMEM((rank * rank, 8, 128), jnp.float32),
            pltpu.VMEM((2 * rank, 24, 128), jnp.float32),
        ],
        compiler_params=SMALL,
        name="gram",
    )(basis)
    parts = jnp.concatenate([got[:, owned_rows * 8, 0, :], gram], axis=0)
    parts = lax.all_to_all(jnp.broadcast_to(parts[None], (blocks, *parts.shape)), ("row", "col"), 0, 0, tiled=True)
    frame_ridge = ridge_share * frames * frame_count
    new_basis, new_coeff = pl.pallas_call(
        functools.partial(final_kernel, pixel_ridge, frame_ridge),
        out_shape=(floats(owned_rows, rank, cols), floats(frames, rank)),
        in_specs=vmem(3),
        out_specs=vmem(2),
        scratch_shapes=[pltpu.VMEM((frame_count + 8, 128), jnp.float32)],
        compiler_params=SMALL,
        name="final",
    )(got.reshape(-1, 128), parts, old_owned)
    return shrunk, new_coeff, new_basis.transpose(1, 0, 2)


def solution(mesh):
    placed = (
        P("frame", "row", "col"),
        P("frame", "row", "col"),
        P("frame", "row", "col"),
        P(None, "row", "col"),
        P("frame", None),
    )
    return jax.shard_map(
        local,
        mesh=mesh,
        in_specs=placed,
        out_specs=(P("frame", "row", "col"), P("frame", None), P(None, ("row", "frame"), "col")),
        check_vma=False,
    )
```

```python
import functools

import jax
import jax.numpy as jnp
from jax import lax
from jax.experimental import pallas as pl
from jax.experimental.pallas import tpu as pltpu
from jax.sharding import PartitionSpec as P

PASSES = 3


relax_rate = 0.8
smooth_weight = 0.5
smooth_floor = 0.25
shrink_level = 0.4
dual_scale = 0.8
ridge_share = 0.1


HIGHEST = lax.Precision.HIGHEST


def iota(shape, dim):
    return lax.broadcasted_iota(jnp.int32, shape, dim)


def dot(a, b):
    return jnp.dot(a, b, precision=HIGHEST, preferred_element_type=jnp.float32)


def eliminated(matrix):
    n = matrix.shape[0]
    wide = (n, 128)
    lanes, rows = iota(wide, 1), iota(wide, 0)
    work = jnp.concatenate([matrix, jnp.zeros((n, 128 - n), jnp.float32)], axis=1)
    work = work + jnp.where(lanes == rows + n, 1.0, 0.0)
    for k in range(0, n, 2):
        col0 = jnp.broadcast_to(work[:, k : k + 1], wide)
        col1 = jnp.broadcast_to(work[:, k + 1 : k + 2], wide)
        row0, row1 = work[k : k + 1, :], work[k + 1 : k + 2, :]
        a, b, d = col0[k : k + 1, :], col1[k : k + 1, :], col1[k + 1 : k + 2, :]
        scale = 1.0 / (a * d - b * b)
        new0 = jnp.broadcast_to((d * row0 - b * row1) * scale, wide)
        new1 = jnp.broadcast_to((a * row1 - b * row0) * scale, wide)
        left = work - col0 * new0 - col1 * new1
        work = jnp.where(rows == k, new0, jnp.where(rows == k + 1, new1, left))
    return work[:, n : 2 * n]


def spread_ranks(rank, width):
    return jnp.where(iota((width, rank), 0) % rank == iota((width, rank), 1), 1.0, 0.0)


def spread_blocks(block, width, count):
    rank = block.shape[0]
    pick = spread_ranks(rank, width)
    full = dot(dot(pick, block), pick.T)
    a, b = iota((width, width), 0) // rank, iota((width, width), 1) // rank
    return jnp.where((a == b) & (a < count), full, 0.0)


def final_kernel(pixel_ridge, ridge, got_ref, parts_ref, old_ref, basis_ref, coeff_ref, coeff_all):
    step = 8 * basis_ref.shape[0] + 1
    slots = got_ref.shape[0] // step
    rank = basis_ref.shape[1]
    rows_owned = basis_ref.shape[0]
    total = parts_ref[0]
    for peer in range(1, parts_ref.shape[0]):
        total = total + parts_ref[peer]
    eye = jnp.where(iota((rank, rank), 0) == iota((rank, rank), 1), 1.0, 0.0)
    inverse = eliminated(total[slots:, 0:rank] + pixel_ridge * eye)
    coeff = dot(total[0:slots], spread_blocks(inverse, 128, 4))
    coeff_all[0:slots] = coeff
    mine = coeff_all[pl.ds(lax.axis_index("frame"), 1), :]
    for f in range(4):
        coeff_ref[f : f + 1, :] = mine[:, f * rank : (f + 1) * rank]
    width = 128
    coeff_t = coeff.T
    full = dot(coeff_t, coeff)
    a, b = iota((width, width), 0) // rank, iota((width, width), 1) // rank
    pick = spread_ranks(rank, width)
    gram = dot(dot(pick.T, jnp.where(a == b, full, 0.0)), pick)
    lines = 8 * slots
    repeat = jnp.where(iota((slots, lines), 0) == iota((slots, lines), 1) // 8, 1.0, 0.0)
    wide = dot(coeff_t, repeat)
    wide = jnp.where(iota((width, lines), 0) // rank == iota((width, lines), 1) % 4, wide, 0.0)
    narrow = wide[0:rank]
    for f in range(1, 4):
        narrow = narrow + wide[f * rank : (f + 1) * rank]
    twice = jnp.concatenate([narrow, narrow], axis=0)
    factor = jnp.where(
        iota((2 * rank, lines), 0) // rank == (iota((2 * rank, lines), 1) // 4) % 2, twice, 0.0
    )
    sums = []
    for i in range(0, rows_owned):
        block = jnp.concatenate(
            [got_ref[n * step + 8 * i : n * step + 8 * (i + 1), :] for n in range(slots)], axis=0
        )
        sums.append(dot(factor, block) + ridge * old_ref[i])
    inverse = spread_blocks(eliminated(gram + ridge * eye), 2 * rank, 2)
    for i in range(rows_owned):
        rows = dot(inverse, sums[i])
        for half in range(2):
            basis_ref[i, :, half * 128 : (half + 1) * 128] = rows[half * rank : (half + 1) * rank]


HALO = 3
GROUP = 12
TOP = 8
FLOOR, SMOOTH, RELAX = smooth_floor, smooth_weight, relax_rate


def lane_of(rows):
    return iota((rows, 128), 1)


def in_lanes(lanes, first, count):
    first = first % 128
    if first + count <= 128:
        return (lanes >= first) & (lanes < first + count)
    return (lanes >= first) | (lanes < first + count - 128)


def goal_rows(coeff, video, multiplier, basis, at, which=range(4)):
    sums = [None] * len(which)
    for r in range(basis.shape[0]):
        image = basis[r, at, :]
        for k, f in enumerate(which):
            term = coeff[f, r] * image
            sums[k] = term if r == 0 else sums[k] + term
    return [video[f, at, :] - sums[k] + dual_scale * multiplier[f, at, :] for k, f in enumerate(which)]


def edge_kernel(coeff, video, multiplier, basis, current, edge, *scratch):
    buffers, sems = scratch[:-1], scratch[-1]
    frames, rows, _ = video.shape
    at = pl.ds(pl.multiple_of((1 - lax.axis_index("row")) * (rows - 8), 8), 8)
    near = [
        pltpu.make_async_copy(ref.at[:, at, :], buf, sems.at[k])
        for k, (ref, buf) in enumerate(zip((video, multiplier, basis, current), buffers))
    ]
    for c in near:
        c.start()
    for c in near:
        c.wait()
    video, multiplier, basis, current = buffers
    edge[0] = current[...]
    for f, value in enumerate(goal_rows(coeff, video, multiplier, basis, slice(0, 8))):
        edge[1, f] = value


def fill_side(forward, coeff, video, multiplier, basis, current, out, ready):
    frames, rows, _ = video.shape
    chunk, piece = 24, rows // len(ready)
    for k in range(HALO):
        out[k] = current[frames - HALO + k if forward else k]
    goals = (frames - 2, frames - 1) if forward else (0, 1)
    for p, wait in enumerate(ready):
        wait()

        def body(c, carry):
            at = pl.ds(pl.multiple_of(p * piece + c * chunk, 8), chunk)
            for k, value in enumerate(goal_rows(coeff, video, multiplier, basis, at, goals)):
                out[HALO + k, at, :] = value
            return carry

        lax.fori_loop(0, piece // chunk, body, 0)


def first_side_kernel(coeff, video, multiplier, basis_in, current, out, basis, sems):
    pieces = sems.shape[0]
    piece = basis.shape[1] // pieces
    copies = []
    for p in range(pieces):
        at = pl.ds(p * piece, piece)
        copies.append(pltpu.make_async_copy(basis_in.at[:, at, :], basis.at[:, at, :], sems.at[p]))
        copies[p].start()
    fill_side(False, coeff, video, multiplier, basis, current, out, [c.wait for c in copies])


def second_side_kernel(coeff, video, multiplier, basis, current, out):
    fill_side(True, coeff, video, multiplier, basis, current, out, [lambda: None])


def strips_kernel(up, down, edge, right, left):
    frames, rows = edge.shape[1], up.shape[1]
    sources = [(up if f > 0 else down, max(f - 1, 0), HALO * GROUP + GROUP * f, 0, f) for f in range(frames)]
    sources += [
        (down if f < 2 else up, HALO + f % 2, HALO * GROUP + GROUP * (f + frames), 1, f) for f in range(frames)
    ]

    def gather(out_at, count, pick):
        lanes = lane_of(count)
        a = jnp.zeros((count, 128), jnp.float32)
        b = a
        for ref, index, base, kind, f in sources:
            first, last = pick(ref, index, kind, f)
            both = jnp.where(lanes < 64, first, last)
            here = in_lanes(lanes, base, GROUP)
            a = jnp.where(here, pltpu.roll(both, (base + 3) % 128, 1), a)
            b = jnp.where(here, pltpu.roll(both, (base + 8) % 128, 1), b)
        right[out_at, :] = a
        left[out_at, :] = b

    def body(c, carry):
        at = pl.ds(pl.multiple_of(c * 32, 32), 32)
        out_at = pl.ds(pl.multiple_of(c * 32 + TOP, 8), 32)
        gather(out_at, 32, lambda ref, i, kind, f: (ref[i, at, 0:128], ref[i, at, 128:256]))
        return carry

    lax.fori_loop(0, rows // 32, body, 0)
    for out_at in (pl.ds(0, 8), pl.ds(rows + TOP, 8)):
        gather(out_at, 8, lambda ref, i, kind, f: (edge[kind, f, :, 0:128], edge[kind, f, :, 128:256]))


def ring_kernel(right, left, from_left, from_right, edge, ring, up, down):
    rows = right.shape[0]
    lanes = lane_of(rows)
    k = (lanes + 128 - HALO * GROUP) % 128 % GROUP
    mine = jnp.where(
        k <= 2,
        from_left[...],
        jnp.where(k <= 5, right[...], jnp.where(k <= 7, left[...], from_right[...])),
    )
    ring[0:rows, :] = mine
    flat = edge.reshape(edge.shape[0] * edge.shape[1] * 8, 256)
    for side in range(2):
        at = rows + side * flat.shape[0]
        ring[at : at + flat.shape[0], :] = flat[:, side * 128 : (side + 1) * 128]
    half = rows // 2
    for out, turn, turn_goal, frame, goal_frame in ((up, 80, 56, 1, 2), (down, 92, 80, 0, 0)):
        part = jnp.where(lanes < 36, pltpu.roll(mine, turn, 1), pltpu.roll(mine, turn_goal, 1))
        out[0:half, :] = jnp.where(lanes[0:half] < 64, part[0:half], pltpu.roll(part[half:], 64, 1))
        for side in range(2):
            cols = slice(side * 128, (side + 1) * 128)
            at = half + side * 40
            for n in range(5):
                tile = edge[0, frame + n, :, cols] if n < 3 else edge[1, goal_frame + n - 3, :, cols]
                out[at + 8 * n : at + 8 * n + 8, :] = tile


def sweep_kernel(
    ridge_part,
    slot_count,
    col_count,
    current,
    before,
    after,
    up,
    down,
    ring,
    ring_before,
    ring_after,
    video,
    multiplier,
    basis,
    coeff,
    shrunk_out,
    sent_out,
    s_a,
    s_b,
    goal,
    strip_a,
    strip_b,
    strip_goal,
    strip_flux,
    flux_f,
    flux_r,
    own_video,
    own_multiplier,
    own_basis,
    residual,
    out,
    sent,
    sums,
    sems,
):
    frames, rows, _ = current.shape
    all_rows = rows + 2 * TOP
    rank = basis.shape[0]
    row, col, slot = lax.axis_index("row"), lax.axis_index("col"), lax.axis_index("frame")
    copies = []

    def copy(src, dst):
        c = pltpu.make_async_copy(src, dst, sems.at[len(copies)])
        c.start()
        copies.append(c)
        return c

    own_at = pl.ds(TOP, rows)
    strip_chunks = [(0, 80), (80, all_rows // 2 - 80)]
    strip_chunks += [(all_rows // 2 + c, count) for c, count in strip_chunks]
    first = []
    for half in range(2):
        at = pl.ds(half * 128, 128)
        for src, start, count, buf, at_frame in (
            (before, 0, HALO, s_a, 0),
            (current, 0, frames, s_a, HALO),
            (after, 0, HALO, s_a, HALO + frames),
            (before, HALO, 2, goal, 0),
            (down, HALO, 2, goal, 2),
            (up, HALO, 2, goal, 4),
            (after, HALO, 2, goal, 6),
        ):
            first.append(copy(src.at[pl.ds(start, count), :, at], buf.at[pl.ds(at_frame, count), half, own_at, :]))

    folded = all_rows // 2
    for c, count in strip_chunks:
        at = slice(c, c + count)
        from_at = slice(c % folded, c % folded + count)
        lanes = lane_of(count)
        mine, prev, nxt = ring[at, :], ring_before[from_at, :], ring_after[from_at, :]
        turn = 64 if c >= folded else 0
        prev_own = pltpu.roll(prev, 64, 1) if turn else prev
        strip_a[at, :] = jnp.where(
            lanes < 36, prev_own, jnp.where(lanes < 84, mine, pltpu.roll(nxt, (84 + turn) % 128, 1))
        )
        strip_goal[at, :] = jnp.where(
            lanes < 36,
            pltpu.roll(prev, (104 + turn) % 128, 1),
            jnp.where(lanes < 84, pltpu.roll(mine, 80, 1), pltpu.roll(nxt, 48 + turn, 1)),
        )
    zero8 = jnp.zeros((8, 128), jnp.float32)
    for buf in (strip_a, strip_b):
        buf[pl.ds(all_rows, 8), :] = zero8
    for half in range(2):
        for g in range(2 * HALO + frames):
            goal_tile = None
            base = folded + half * 40
            if g < HALO:
                tile = ring_before[base + 8 * g : base + 8 * g + 8, :]
                if g >= 1:
                    goal_tile = ring_before[base + 8 * (g + 2) : base + 8 * (g + 2) + 8, :]
            elif g < HALO + frames:
                at = all_rows + half * 2 * frames * 8 + (g - HALO) * 8
                tile, goal_tile = ring[at : at + 8, :], ring[at + frames * 8 : at + frames * 8 + 8, :]
            else:
                n = g - HALO - frames
                tile = ring_after[base + 8 * n : base + 8 * n + 8, :]
                if n <= 1:
                    goal_tile = ring_after[base + 8 * (n + 3) : base + 8 * (n + 3) + 8, :]
            s_a[g, half, 0:TOP, :] = tile
            s_a[g, half, pl.ds(TOP + rows, 8), :] = tile
            s_a[g, half, pl.ds(all_rows, 8), :] = zero8
            s_b[g, half, pl.ds(all_rows, 8), :] = zero8
            if goal_tile is not None:
                goal[g - 1, half, 0:TOP, :] = goal_tile
                goal[g - 1, half, pl.ds(TOP + rows, 8), :] = goal_tile

    def first_row_last(value, count):
        return value[count - 1 : count, :]

    def down_one(value, carry, count):
        moved = pltpu.roll(value, 1, 0)
        return jnp.where(iota((count, 128), 0) == 0, jnp.broadcast_to(carry, (count, 128)), moved)

    def strip_sweep(old, new, flux_at):
        for c, count in strip_chunks:
            lanes = lane_of(count)
            k = lanes % GROUP
            s = old[c : c + count, :]
            s = jnp.where((slot == 0) & in_lanes(lanes, 24, 12), pltpu.roll(s, 116, 1), s)
            s = jnp.where((slot == slots_end) & in_lanes(lanes, 84, 12), pltpu.roll(s, 12, 1), s)
            s = jnp.where((col == 0) & (k == 2), pltpu.roll(s, 127, 1), s)
            s = jnp.where((col == cols_end) & (k == 8), pltpu.roll(s, 1, 1), s)
            old[c : c + count, :] = s

        @pl.when(row == 0)
        def _():
            old[TOP - 1 : TOP, :] = old[TOP : TOP + 1, :]

        @pl.when(row == 1)
        def _():
            old[TOP + rows : TOP + rows + 1, :] = old[TOP + rows - 1 : TOP + rows, :]

        carry = jnp.zeros((1, 128), jnp.float32)
        for c, count in strip_chunks:
            s = old[c : c + count, :]
            pf = pltpu.roll(s, 116, 1) - s
            pr = old[c + 1 : c + 1 + count, :] - s
            pc = pltpu.roll(s, 127, 1) - s
            weight = lax.rsqrt(FLOOR + pf * pf + pr * pr + pc * pc)
            ff, fr, fc = pf * weight, pr * weight, pc * weight
            k = lane_of(count) % GROUP
            strip_flux[flux_at, c : c + count, :] = jnp.where(k == 8, s, pltpu.roll(fc, 7, 1))
            spread = (
                (ff - pltpu.roll(ff, 12, 1)) + (fr - down_one(fr, carry, count)) + (fc - pltpu.roll(fc, 1, 1))
            )
            carry = first_row_last(fr, count)
            new[c : c + count, :] = s + RELAX * (strip_goal[c : c + count, :] - s + SMOOTH * spread)

    slots_end, cols_end = slot_count - 1, col_count - 1
    for half in range(2):
        flux_r[half, 0:8, :] = zero8
    strip_sweep(strip_a, strip_b, 0)
    strip_sweep(strip_b, strip_a, 1)
    strip_sweep(strip_a, strip_b, 2)

    for c in first:
        c.wait()
    later = [copy(video, own_video), copy(multiplier, own_multiplier), copy(basis, own_basis)]

    chunks = [(c, min(64, all_rows - c)) for c in range(0, all_rows, 64)]

    def edges(old):
        @pl.when(slot == 0)
        def _():
            old[HALO - 1] = old[HALO]

        @pl.when(slot == slots_end)
        def _():
            old[HALO + frames] = old[HALO + frames - 1]

        @pl.when(row == 0)
        def _():
            for g in range(2 * HALO + frames):
                for half in range(2):
                    old[g, half, TOP - 1 : TOP, :] = old[g, half, TOP : TOP + 1, :]

        @pl.when(row == 1)
        def _():
            end = TOP + rows
            for g in range(2 * HALO + frames):
                for half in range(2):
                    old[g, half, end : end + 1, :] = old[g, half, end - 1 : end, :]

    last_keep = jnp.where((lane_of(8)[0:1] == 127) & (col == cols_end), 0.0, 1.0)

    def main_sweep(old, new, flux_at, g_first, g_count):
        edges(old)

        def body(i, carry0):
            g = g_first + i
            turn = (119 + 12 * 128 - 12 * g) % 128
            goal_at = jnp.maximum(g - 1, 0)
            for c, count in chunks:
                lanes = lane_of(count)
                at = pl.ds(c, count)
                next_at = pl.ds(c + 1, count)
                s = [old[g, half, at, :] for half in range(2)]
                turned = [pltpu.roll(x, 127, 1) for x in s]
                outside = pltpu.roll(strip_flux[flux_at, at, :], turn, 1)
                ahead = [
                    jnp.where(lanes == 127, turned[1], turned[0]),
                    jnp.where(lanes == 127, outside, turned[1]),
                ]
                fc, fr, ff = [], [], []
                for half in range(2):
                    x = s[half]
                    pf = old[g + 1, half, at, :] - x
                    pr = old[g, half, next_at, :] - x
                    pc = ahead[half] - x
                    if half == 1:
                        pc = pc * last_keep
                    weight = lax.rsqrt(FLOOR + pf * pf + pr * pr + pc * pc)
                    ff.append(pf * weight)
                    fr.append(pr * weight)
                    flux_r[half, pl.ds(c + 8, count), :] = fr[half]
                    fc.append(pc * weight)
                turned = [pltpu.roll(x, 1, 1) for x in fc]
                behind = [
                    jnp.where(lanes == 0, outside, turned[0]),
                    jnp.where(lanes == 0, turned[0], turned[1]),
                ]
                for half in range(2):
                    x = s[half]
                    spread = (
                        (ff[half] - flux_f[half, at, :])
                        + (fr[half] - flux_r[half, pl.ds(c + 7, count), :])
                        + (fc[half] - behind[half])
                    )
                    flux_f[half, at, :] = ff[half]
                    new[g, half, at, :] = x + RELAX * (goal[goal_at, half, at, :] - x + SMOOTH * spread)
            return carry0

        lax.fori_loop(0, g_count, body, 0)

    main_sweep(s_a, s_b, 0, 0, 9)
    main_sweep(s_b, s_a, 1, 1, 7)
    main_sweep(s_a, s_b, 2, 2, 5)

    for c in later:
        c.wait()
    sums[...] = jnp.zeros_like(sums)

    def finish(c, carry):
        chunk = 16
        at = pl.ds(pl.multiple_of(c * chunk, chunk), chunk)
        in_at = pl.ds(pl.multiple_of(c * chunk + TOP, 8), chunk)
        parts = []
        for f in range(frames):
            for half in range(2):
                cols = slice(half * 128, (half + 1) * 128)
                s = s_b[HALO + f, half, in_at, :]
                shrunk = s - jnp.clip(s, -shrink_level, shrink_level)
                out[f, at, cols] = shrunk
                r = own_video[f, at, cols] + dual_scale * own_multiplier[f, at, cols] - shrunk
                residual[half * frames + f, at, :] = r
                parts.append(r)
        for r in range(rank):
            images = [own_basis[r, at, half * 128 : (half + 1) * 128] for half in range(2)]
            for f in range(frames):
                term = images[0] * parts[2 * f] + images[1] * parts[2 * f + 1]
                sums[f * rank + r] += term[0:8] + term[8:16]
        return carry

    lax.fori_loop(0, rows // 16, finish, 0)
    done = copy(out, shrunk_out)
    lines = jnp.sum(sums[...], axis=1)
    total = lax.dot_general(
        jnp.ones((8, 128), jnp.float32),
        lines,
        (((1,), (1,)), ((), ())),
        precision=HIGHEST,
        preferred_element_type=jnp.float32,
    )
    cross = jnp.concatenate([total[0:1] + ridge_part * coeff[...], jnp.zeros((1, 64), jnp.float32)], axis=1)
    owned = rows // slot_count
    chunk_rows = owned * 8 + 1

    def pack(j, carry):
        for f in range(frames):
            for half in range(2):
                sent[pl.ds(j * chunk_rows + half * frames + f, owned, stride=8), :] = residual[
                    half * frames + f, pl.ds(j * owned, owned), :
                ]
        sent[pl.ds(j * chunk_rows + owned * 8, 1), :] = cross
        return carry

    done = [done]
    group = slot_count // 4
    for n in range(4):
        lax.fori_loop(n * group, (n + 1) * group, pack, 0)
        at = pl.ds(n * group * chunk_rows, group * chunk_rows)
        done.append(copy(sent.at[at], sent_out.at[at]))
    for c in done:
        c.wait()


def gram_kernel(slot_count, basis, out, old, sums, window):
    rank, rows, _ = basis.shape
    sums[...] = jnp.zeros_like(sums)

    def body(c, carry):
        at = pl.ds(pl.multiple_of(c * 8, 8), 8)
        images = [[basis[r, at, half * 128 : (half + 1) * 128] for half in range(2)] for r in range(rank)]
        for r in range(rank):
            for q in range(r, rank):
                sums[r * rank + q] += images[r][0] * images[q][0] + images[r][1] * images[q][1]
        return carry

    lax.fori_loop(0, rows // 8, body, 0)
    owned = rows // slot_count
    start = pl.multiple_of(lax.axis_index("frame") * owned // 8 * 8, 8)
    shift = lax.axis_index("frame") * owned - start
    flat = old.reshape(old.shape[0] * 2 * rank, 128)
    for half in range(2):
        for r in range(rank):
            window[half * rank + r, 0:16] = basis[r, pl.ds(start, 16), half * 128 : (half + 1) * 128]
            flat[pl.ds(half * rank + r, owned, stride=2 * rank), :] = window[half * rank + r, pl.ds(shift, owned), :]
    ones = jnp.ones((128, 128), jnp.float32)
    for r in range(rank):
        lines = jnp.concatenate(
            [jnp.sum(sums[min(r, q) * rank + max(r, q)], axis=0, keepdims=True) for q in range(rank)], axis=0
        )
        totals = dot(lines, ones)
        picked = jnp.where(iota((rank, 128), 0) == iota((rank, 128), 1), totals, 0.0)
        out[r : r + 1, :] = jnp.sum(picked, axis=0, keepdims=True)


def vmem(count):
    return [pl.BlockSpec(memory_space=pltpu.VMEM)] * count


def smem():
    return pl.BlockSpec(memory_space=pltpu.SMEM)


def anywhere(count):
    return [pl.BlockSpec(memory_space=pltpu.HBM)] * count


def floats(*shape):
    return jax.ShapeDtypeStruct(shape, jnp.float32)


LARGE = pltpu.CompilerParams(vmem_limit_bytes=28 * 1024 * 1024)
SMALL = pltpu.CompilerParams(vmem_limit_bytes=20 * 1024 * 1024)


def in_hbm(*shape):
    return pltpu.HBM(shape, jnp.float32)


def local(video, multiplier, foreground, basis, coefficients):
    plain = (video, multiplier)
    video, multiplier, basis = (pltpu.with_memory_space_constraint(x, pltpu.HBM) for x in (video, multiplier, basis))
    frames, rows, cols = video.shape
    rank = basis.shape[0]
    frame_count = lax.axis_size("frame")
    row_count = lax.axis_size("row")
    col_count = lax.axis_size("col")
    blocks = row_count * col_count
    all_rows = rows + 2 * TOP
    to_next = [(i, i + 1) for i in range(frame_count - 1)]
    to_previous = [(b, a) for a, b in to_next]
    to_right = [(i, i + 1) for i in range(col_count - 1)]
    to_left = [(b, a) for a, b in to_right]

    edge = pl.pallas_call(
        edge_kernel,
        out_shape=floats(2, frames, 8, cols),
        in_specs=[smem()] + anywhere(4),
        out_specs=vmem(1)[0],
        scratch_shapes=[pltpu.VMEM((n, 8, cols), jnp.float32) for n in (frames, frames, rank, frames)]
        + [pltpu.SemaphoreType.DMA((4,))],
        name="edge",
    )(coefficients, video, multiplier, basis, foreground)
    edge = lax.ppermute(edge, "row", [(0, 1), (1, 0)])
    down, images = pl.pallas_call(
        first_side_kernel,
        out_shape=(pltpu.VMEM((HALO + 2, rows, cols), jnp.float32), pltpu.VMEM(basis.shape, jnp.float32)),
        in_specs=[smem()] + vmem(2) + anywhere(1) + vmem(1),
        out_specs=vmem(2),
        scratch_shapes=[pltpu.SemaphoreType.DMA((6,))],
        compiler_params=SMALL,
        name="first_side",
    )(coefficients, *plain, basis, foreground)
    up = pl.pallas_call(
        second_side_kernel,
        out_shape=pltpu.VMEM((HALO + 2, rows, cols), jnp.float32),
        in_specs=[smem()] + vmem(4),
        out_specs=vmem(1)[0],
        compiler_params=SMALL,
        name="second_side",
    )(coefficients, *plain, images, foreground)
    up, edge = lax.optimization_barrier((up, edge))
    before = lax.ppermute(up, "frame", to_next)
    after = lax.ppermute(down, "frame", to_previous)
    right, left = pl.pallas_call(
        strips_kernel,
        out_shape=(floats(all_rows, 128), floats(all_rows, 128)),
        in_specs=vmem(3),
        out_specs=vmem(2),
        compiler_params=SMALL,
        name="strips",
    )(up, down, edge)
    from_left = lax.ppermute(right, "col", to_right)
    from_right = lax.ppermute(left, "col", to_left)
    folded = all_rows // 2
    ring, ring_up, ring_down = pl.pallas_call(
        ring_kernel,
        out_shape=(floats(all_rows + 16 * frames * 2, 128), floats(folded + 80, 128), floats(folded + 80, 128)),
        in_specs=vmem(5),
        out_specs=vmem(3),
        compiler_params=SMALL,
        name="ring",
    )(right, left, from_left, from_right, edge)
    ring_before = lax.ppermute(ring_up, "frame", to_next)
    ring_after = lax.ppermute(ring_down, "frame", to_previous)

    pixel_ridge = ridge_share * rows * cols * blocks
    owned_rows = rows // frame_count
    main = (2 * HALO + frames, 2, all_rows + 8, 128)
    strip = (all_rows + 8, 128)
    scratch = [
        main,
        main,
        (2 * HALO + frames - 2, 2, all_rows, 128),
        strip,
        strip,
        (all_rows, 128),
        (3, all_rows, 128),
        (2, all_rows, 128),
        (2, all_rows + 8, 128),
        video.shape,
        video.shape,
        basis.shape,
        (2 * frames, rows + 16, 128),
        video.shape,
        (frame_count * (owned_rows * 8 + 1) + 64, 128),
        (frames * rank, 8, 128),
    ]
    shrunk, sent = pl.pallas_call(
        functools.partial(sweep_kernel, pixel_ridge / blocks, frame_count, col_count),
        out_shape=(in_hbm(frames, rows, cols), in_hbm(frame_count * (owned_rows * 8 + 1), 128)),
        in_specs=anywhere(5) + vmem(3) + anywhere(3) + vmem(1),
        out_specs=anywhere(2),
        scratch_shapes=[pltpu.VMEM(s, jnp.float32) for s in scratch] + [pltpu.SemaphoreType.DMA((22,))],
        compiler_params=LARGE,
        name="sweeps",
    )(
        foreground,
        before,
        after,
        up,
        down,
        ring,
        ring_before,
        ring_after,
        video,
        multiplier,
        basis,
        coefficients.reshape(1, frames * rank),
    )
    got = lax.all_to_all(sent.reshape(frame_count, owned_rows * 8 + 1, 1, 128), "frame", 0, 0, tiled=True)
    basis, _ = lax.optimization_barrier((basis, sent))
    gram, old_owned = pl.pallas_call(
        functools.partial(gram_kernel, frame_count),
        out_shape=(floats(rank, 128), floats(16, 2 * rank, 128)),
        in_specs=vmem(1),
        out_specs=vmem(2),
        scratch_shapes=[
            pltpu.VMEM((rank * rank, 8, 128), jnp.float32),
            pltpu.VMEM((2 * rank, 24, 128), jnp.float32),
        ],
        compiler_params=SMALL,
        name="gram",
    )(basis)
    parts = jnp.concatenate([got[:, owned_rows * 8, 0, :], gram], axis=0)
    parts = lax.all_to_all(jnp.broadcast_to(parts[None], (blocks, *parts.shape)), ("row", "col"), 0, 0, tiled=True)
    frame_ridge = ridge_share * frames * frame_count
    new_basis, new_coeff = pl.pallas_call(
        functools.partial(final_kernel, pixel_ridge, frame_ridge),
        out_shape=(floats(owned_rows, rank, cols), floats(frames, rank)),
        in_specs=vmem(3),
        out_specs=vmem(2),
        scratch_shapes=[pltpu.VMEM((frame_count + 8, 128), jnp.float32)],
        compiler_params=SMALL,
        name="final",
    )(got.reshape(-1, 128), parts, old_owned)
    return shrunk, new_coeff, new_basis.transpose(1, 0, 2)


def solution(mesh):
    placed = (
        P("frame", "row", "col"),
        P("frame", "row", "col"),
        P("frame", "row", "col"),
        P(None, "row", "col"),
        P("frame", None),
    )
    return jax.shard_map(
        local,
        mesh=mesh,
        in_specs=placed,
        out_specs=(P("frame", "row", "col"), P("frame", None), P(None, ("row", "frame"), "col")),
        check_vma=False,
    )
```

```python
import functools

import jax
import jax.numpy as jnp
from jax import lax
from jax.experimental import pallas as pl
from jax.experimental.pallas import tpu as pltpu
from jax.sharding import PartitionSpec as P

PASSES = 3


relax_rate = 0.8
smooth_weight = 0.5
smooth_floor = 0.25
shrink_level = 0.4
dual_scale = 0.8
ridge_share = 0.1


HIGHEST = lax.Precision.HIGHEST


def iota(shape, dim):
    return lax.broadcasted_iota(jnp.int32, shape, dim)


def dot(a, b):
    return jnp.dot(a, b, precision=HIGHEST, preferred_element_type=jnp.float32)


def eliminated(matrix):
    n = matrix.shape[0]
    wide = (n, 128)
    lanes, rows = iota(wide, 1), iota(wide, 0)
    work = jnp.concatenate([matrix, jnp.zeros((n, 128 - n), jnp.float32)], axis=1)
    work = work + jnp.where(lanes == rows + n, 1.0, 0.0)
    for k in range(0, n, 2):
        col0 = jnp.broadcast_to(work[:, k : k + 1], wide)
        col1 = jnp.broadcast_to(work[:, k + 1 : k + 2], wide)
        row0, row1 = work[k : k + 1, :], work[k + 1 : k + 2, :]
        a, b, d = col0[k : k + 1, :], col1[k : k + 1, :], col1[k + 1 : k + 2, :]
        scale = 1.0 / (a * d - b * b)
        new0 = jnp.broadcast_to((d * row0 - b * row1) * scale, wide)
        new1 = jnp.broadcast_to((a * row1 - b * row0) * scale, wide)
        left = work - col0 * new0 - col1 * new1
        work = jnp.where(rows == k, new0, jnp.where(rows == k + 1, new1, left))
    return work[:, n : 2 * n]


def spread_ranks(rank, width):
    return jnp.where(iota((width, rank), 0) % rank == iota((width, rank), 1), 1.0, 0.0)


def spread_blocks(block, width, count):
    rank = block.shape[0]
    pick = spread_ranks(rank, width)
    full = dot(dot(pick, block), pick.T)
    a, b = iota((width, width), 0) // rank, iota((width, width), 1) // rank
    return jnp.where((a == b) & (a < count), full, 0.0)


def final_kernel(pixel_ridge, ridge, got_ref, parts_ref, old_ref, basis_ref, coeff_ref, coeff_all):
    step = 8 * basis_ref.shape[0] + 1
    slots = got_ref.shape[0] // step
    rank = basis_ref.shape[1]
    rows_owned = basis_ref.shape[0]
    total = parts_ref[0]
    for peer in range(1, parts_ref.shape[0]):
        total = total + parts_ref[peer]
    eye = jnp.where(iota((rank, rank), 0) == iota((rank, rank), 1), 1.0, 0.0)
    inverse = eliminated(total[slots:, 0:rank] + pixel_ridge * eye)
    coeff = dot(total[0:slots], spread_blocks(inverse, 128, 4))
    coeff_all[0:slots] = coeff
    mine = coeff_all[pl.ds(lax.axis_index("frame"), 1), :]
    for f in range(4):
        coeff_ref[f : f + 1, :] = mine[:, f * rank : (f + 1) * rank]
    width = 128
    coeff_t = coeff.T
    full = dot(coeff_t, coeff)
    a, b = iota((width, width), 0) // rank, iota((width, width), 1) // rank
    pick = spread_ranks(rank, width)
    gram = dot(dot(pick.T, jnp.where(a == b, full, 0.0)), pick)
    lines = 8 * slots
    repeat = jnp.where(iota((slots, lines), 0) == iota((slots, lines), 1) // 8, 1.0, 0.0)
    wide = dot(coeff_t, repeat)
    wide = jnp.where(iota((width, lines), 0) // rank == iota((width, lines), 1) % 4, wide, 0.0)
    narrow = wide[0:rank]
    for f in range(1, 4):
        narrow = narrow + wide[f * rank : (f + 1) * rank]
    twice = jnp.concatenate([narrow, narrow], axis=0)
    factor = jnp.where(
        iota((2 * rank, lines), 0) // rank == (iota((2 * rank, lines), 1) // 4) % 2, twice, 0.0
    )
    sums = []
    for i in range(0, rows_owned):
        block = jnp.concatenate(
            [got_ref[n * step + 8 * i : n * step + 8 * (i + 1), :] for n in range(slots)], axis=0
        )
        sums.append(dot(factor, block) + ridge * old_ref[i])
    inverse = spread_blocks(eliminated(gram + ridge * eye), 2 * rank, 2)
    for i in range(rows_owned):
        rows = dot(inverse, sums[i])
        for half in range(2):
            basis_ref[i, :, half * 128 : (half + 1) * 128] = rows[half * rank : (half + 1) * rank]


HALO = 3
GROUP = 12
TOP = 8
FLOOR, SMOOTH, RELAX = smooth_floor, smooth_weight, relax_rate


def lane_of(rows):
    return iota((rows, 128), 1)


def in_lanes(lanes, first, count):
    first = first % 128
    if first + count <= 128:
        return (lanes >= first) & (lanes < first + count)
    return (lanes >= first) | (lanes < first + count - 128)


def goal_rows(coeff, video, multiplier, basis, at, which=range(4)):
    sums = [None] * len(which)
    for r in range(basis.shape[0]):
        image = basis[r, at, :]
        for k, f in enumerate(which):
            term = coeff[f, r] * image
            sums[k] = term if r == 0 else sums[k] + term
    return [video[f, at, :] - sums[k] + dual_scale * multiplier[f, at, :] for k, f in enumerate(which)]


def edge_kernel(coeff, video, multiplier, basis, current, edge, *scratch):
    buffers, sems = scratch[:-1], scratch[-1]
    frames, rows, _ = video.shape
    at = pl.ds(pl.multiple_of((1 - lax.axis_index("row")) * (rows - 8), 8), 8)
    near = [
        pltpu.make_async_copy(ref.at[:, at, :], buf, sems.at[k])
        for k, (ref, buf) in enumerate(zip((video, multiplier, basis, current), buffers))
    ]
    for c in near:
        c.start()
    for c in near:
        c.wait()
    video, multiplier, basis, current = buffers
    edge[0] = current[...]
    for f, value in enumerate(goal_rows(coeff, video, multiplier, basis, slice(0, 8))):
        edge[1, f] = value


def fill_side(forward, coeff, video, multiplier, basis, current, out, ready):
    frames, rows, _ = video.shape
    chunk, piece = 24, rows // len(ready)
    for k in range(HALO):
        out[k] = current[frames - HALO + k if forward else k]
    goals = (frames - 2, frames - 1) if forward else (0, 1)
    for p, wait in enumerate(ready):
        wait()

        def body(c, carry):
            at = pl.ds(pl.multiple_of(p * piece + c * chunk, 8), chunk)
            for k, value in enumerate(goal_rows(coeff, video, multiplier, basis, at, goals)):
                out[HALO + k, at, :] = value
            return carry

        lax.fori_loop(0, piece // chunk, body, 0)


def first_side_kernel(coeff, video, multiplier, basis_in, current, out, basis, sems):
    pieces = sems.shape[0]
    piece = basis.shape[1] // pieces
    copies = []
    for p in range(pieces):
        at = pl.ds(p * piece, piece)
        copies.append(pltpu.make_async_copy(basis_in.at[:, at, :], basis.at[:, at, :], sems.at[p]))
        copies[p].start()
    fill_side(False, coeff, video, multiplier, basis, current, out, [c.wait for c in copies])


def second_side_kernel(coeff, video, multiplier, basis, current, out):
    fill_side(True, coeff, video, multiplier, basis, current, out, [lambda: None])


def strips_kernel(up, down, edge, right, left):
    frames, rows = edge.shape[1], up.shape[1]
    sources = [(up if f > 0 else down, max(f - 1, 0), HALO * GROUP + GROUP * f, 0, f) for f in range(frames)]
    sources += [
        (down if f < 2 else up, HALO + f % 2, HALO * GROUP + GROUP * (f + frames), 1, f) for f in range(frames)
    ]

    def gather(out_at, count, pick):
        lanes = lane_of(count)
        a = jnp.zeros((count, 128), jnp.float32)
        b = a
        for ref, index, base, kind, f in sources:
            first, last = pick(ref, index, kind, f)
            both = jnp.where(lanes < 64, first, last)
            here = in_lanes(lanes, base, GROUP)
            a = jnp.where(here, pltpu.roll(both, (base + 3) % 128, 1), a)
            b = jnp.where(here, pltpu.roll(both, (base + 8) % 128, 1), b)
        right[out_at, :] = a
        left[out_at, :] = b

    def body(c, carry):
        at = pl.ds(pl.multiple_of(c * 32, 32), 32)
        out_at = pl.ds(pl.multiple_of(c * 32 + TOP, 8), 32)
        gather(out_at, 32, lambda ref, i, kind, f: (ref[i, at, 0:128], ref[i, at, 128:256]))
        return carry

    lax.fori_loop(0, rows // 32, body, 0)
    for out_at in (pl.ds(0, 8), pl.ds(rows + TOP, 8)):
        gather(out_at, 8, lambda ref, i, kind, f: (edge[kind, f, :, 0:128], edge[kind, f, :, 128:256]))


def ring_kernel(right, left, from_left, from_right, edge, ring, up, down):
    rows = right.shape[0]
    lanes = lane_of(rows)
    k = (lanes + 128 - HALO * GROUP) % 128 % GROUP
    mine = jnp.where(
        k <= 2,
        from_left[...],
        jnp.where(k <= 5, right[...], jnp.where(k <= 7, left[...], from_right[...])),
    )
    ring[0:rows, :] = mine
    flat = edge.reshape(edge.shape[0] * edge.shape[1] * 8, 256)
    for side in range(2):
        at = rows + side * flat.shape[0]
        ring[at : at + flat.shape[0], :] = flat[:, side * 128 : (side + 1) * 128]
    half = rows // 2
    for out, turn, turn_goal, frame, goal_frame in ((up, 80, 56, 1, 2), (down, 92, 80, 0, 0)):
        part = jnp.where(lanes < 36, pltpu.roll(mine, turn, 1), pltpu.roll(mine, turn_goal, 1))
        out[0:half, :] = jnp.where(lanes[0:half] < 64, part[0:half], pltpu.roll(part[half:], 64, 1))
        for side in range(2):
            cols = slice(side * 128, (side + 1) * 128)
            at = half + side * 40
            for n in range(5):
                tile = edge[0, frame + n, :, cols] if n < 3 else edge[1, goal_frame + n - 3, :, cols]
                out[at + 8 * n : at + 8 * n + 8, :] = tile


def sweep_kernel(
    ridge_part,
    slot_count,
    col_count,
    current,
    before,
    after,
    up,
    down,
    ring,
    ring_before,
    ring_after,
    video,
    multiplier,
    basis,
    coeff,
    shrunk_out,
    sent_out,
    s_a,
    s_b,
    goal,
    strip_a,
    strip_b,
    strip_goal,
    strip_flux,
    flux_f,
    flux_r,
    own_video,
    own_multiplier,
    own_basis,
    residual,
    out,
    sent,
    sums,
    sems,
):
    frames, rows, _ = current.shape
    all_rows = rows + 2 * TOP
    rank = basis.shape[0]
    row, col, slot = lax.axis_index("row"), lax.axis_index("col"), lax.axis_index("frame")
    copies = []

    def copy(src, dst):
        c = pltpu.make_async_copy(src, dst, sems.at[len(copies)])
        c.start()
        copies.append(c)
        return c

    own_at = pl.ds(TOP, rows)
    strip_chunks = [(0, 80), (80, all_rows // 2 - 80)]
    strip_chunks += [(all_rows // 2 + c, count) for c, count in strip_chunks]
    first = []
    for half in range(2):
        at = pl.ds(half * 128, 128)
        for src, start, count, buf, at_frame in (
            (before, 0, HALO, s_a, 0),
            (current, 0, frames, s_a, HALO),
            (after, 0, HALO, s_a, HALO + frames),
            (before, HALO, 2, goal, 0),
            (down, HALO, 2, goal, 2),
            (up, HALO, 2, goal, 4),
            (after, HALO, 2, goal, 6),
        ):
            first.append(copy(src.at[pl.ds(start, count), :, at], buf.at[pl.ds(at_frame, count), half, own_at, :]))

    folded = all_rows // 2
    for c, count in strip_chunks:
        at = slice(c, c + count)
        from_at = slice(c % folded, c % folded + count)
        lanes = lane_of(count)
        mine, prev, nxt = ring[at, :], ring_before[from_at, :], ring_after[from_at, :]
        turn = 64 if c >= folded else 0
        prev_own = pltpu.roll(prev, 64, 1) if turn else prev
        strip_a[at, :] = jnp.where(
            lanes < 36, prev_own, jnp.where(lanes < 84, mine, pltpu.roll(nxt, (84 + turn) % 128, 1))
        )
        strip_goal[at, :] = jnp.where(
            lanes < 36,
            pltpu.roll(prev, (104 + turn) % 128, 1),
            jnp.where(lanes < 84, pltpu.roll(mine, 80, 1), pltpu.roll(nxt, 48 + turn, 1)),
        )
    zero8 = jnp.zeros((8, 128), jnp.float32)
    for buf in (strip_a, strip_b):
        buf[pl.ds(all_rows, 8), :] = zero8
    for half in range(2):
        for g in range(2 * HALO + frames):
            goal_tile = None
            base = folded + half * 40
            if g < HALO:
                tile = ring_before[base + 8 * g : base + 8 * g + 8, :]
                if g >= 1:
                    goal_tile = ring_before[base + 8 * (g + 2) : base + 8 * (g + 2) + 8, :]
            elif g < HALO + frames:
                at = all_rows + half * 2 * frames * 8 + (g - HALO) * 8
                tile, goal_tile = ring[at : at + 8, :], ring[at + frames * 8 : at + frames * 8 + 8, :]
            else:
                n = g - HALO - frames
                tile = ring_after[base + 8 * n : base + 8 * n + 8, :]
                if n <= 1:
                    goal_tile = ring_after[base + 8 * (n + 3) : base + 8 * (n + 3) + 8, :]
            s_a[g, half, 0:TOP, :] = tile
            s_a[g, half, pl.ds(TOP + rows, 8), :] = tile
            s_a[g, half, pl.ds(all_rows, 8), :] = zero8
            s_b[g, half, pl.ds(all_rows, 8), :] = zero8
            if goal_tile is not None:
                goal[g - 1, half, 0:TOP, :] = goal_tile
                goal[g - 1, half, pl.ds(TOP + rows, 8), :] = goal_tile

    def first_row_last(value, count):
        return value[count - 1 : count, :]

    def down_one(value, carry, count):
        moved = pltpu.roll(value, 1, 0)
        return jnp.where(iota((count, 128), 0) == 0, jnp.broadcast_to(carry, (count, 128)), moved)

    def strip_sweep(old, new, flux_at):
        for c, count in strip_chunks:
            lanes = lane_of(count)
            k = lanes % GROUP
            s = old[c : c + count, :]
            s = jnp.where((slot == 0) & in_lanes(lanes, 24, 12), pltpu.roll(s, 116, 1), s)
            s = jnp.where((slot == slots_end) & in_lanes(lanes, 84, 12), pltpu.roll(s, 12, 1), s)
            s = jnp.where((col == 0) & (k == 2), pltpu.roll(s, 127, 1), s)
            s = jnp.where((col == cols_end) & (k == 8), pltpu.roll(s, 1, 1), s)
            old[c : c + count, :] = s

        @pl.when(row == 0)
        def _():
            old[TOP - 1 : TOP, :] = old[TOP : TOP + 1, :]

        @pl.when(row == 1)
        def _():
            old[TOP + rows : TOP + rows + 1, :] = old[TOP + rows - 1 : TOP + rows, :]

        carry = jnp.zeros((1, 128), jnp.float32)
        for c, count in strip_chunks:
            s = old[c : c + count, :]
            pf = pltpu.roll(s, 116, 1) - s
            pr = old[c + 1 : c + 1 + count, :] - s
            pc = pltpu.roll(s, 127, 1) - s
            weight = lax.rsqrt(FLOOR + pf * pf + pr * pr + pc * pc)
            ff, fr, fc = pf * weight, pr * weight, pc * weight
            k = lane_of(count) % GROUP
            strip_flux[flux_at, c : c + count, :] = jnp.where(k == 8, s, pltpu.roll(fc, 7, 1))
            spread = (
                (ff - pltpu.roll(ff, 12, 1)) + (fr - down_one(fr, carry, count)) + (fc - pltpu.roll(fc, 1, 1))
            )
            carry = first_row_last(fr, count)
            new[c : c + count, :] = s + RELAX * (strip_goal[c : c + count, :] - s + SMOOTH * spread)

    slots_end, cols_end = slot_count - 1, col_count - 1
    for half in range(2):
        flux_r[half, 0:8, :] = zero8
    strip_sweep(strip_a, strip_b, 0)
    strip_sweep(strip_b, strip_a, 1)
    strip_sweep(strip_a, strip_b, 2)

    for c in first:
        c.wait()
    later = [copy(video, own_video), copy(multiplier, own_multiplier), copy(basis, own_basis)]

    chunks = [(c, min(64, all_rows - c)) for c in range(0, all_rows, 64)]

    def edges(old):
        @pl.when(slot == 0)
        def _():
            old[HALO - 1] = old[HALO]

        @pl.when(slot == slots_end)
        def _():
            old[HALO + frames] = old[HALO + frames - 1]

        @pl.when(row == 0)
        def _():
            for g in range(2 * HALO + frames):
                for half in range(2):
                    old[g, half, TOP - 1 : TOP, :] = old[g, half, TOP : TOP + 1, :]

        @pl.when(row == 1)
        def _():
            end = TOP + rows
            for g in range(2 * HALO + frames):
                for half in range(2):
                    old[g, half, end : end + 1, :] = old[g, half, end - 1 : end, :]

    last_keep = jnp.where((lane_of(8)[0:1] == 127) & (col == cols_end), 0.0, 1.0)

    def main_sweep(old, new, flux_at, g_first, g_count):
        edges(old)

        def body(i, carry0):
            g = g_first + i
            turn = (119 + 12 * 128 - 12 * g) % 128
            goal_at = jnp.maximum(g - 1, 0)
            for c, count in chunks:
                lanes = lane_of(count)
                at = pl.ds(c, count)
                next_at = pl.ds(c + 1, count)
                s = [old[g, half, at, :] for half in range(2)]
                turned = [pltpu.roll(x, 127, 1) for x in s]
                outside = pltpu.roll(strip_flux[flux_at, at, :], turn, 1)
                ahead = [
                    jnp.where(lanes == 127, turned[1], turned[0]),
                    jnp.where(lanes == 127, outside, turned[1]),
                ]
                fc, fr, ff = [], [], []
                for half in range(2):
                    x = s[half]
                    pf = old[g + 1, half, at, :] - x
                    pr = old[g, half, next_at, :] - x
                    pc = ahead[half] - x
                    if half == 1:
                        pc = pc * last_keep
                    weight = lax.rsqrt(FLOOR + pf * pf + pr * pr + pc * pc)
                    ff.append(pf * weight)
                    fr.append(pr * weight)
                    flux_r[half, pl.ds(c + 8, count), :] = fr[half]
                    fc.append(pc * weight)
                turned = [pltpu.roll(x, 1, 1) for x in fc]
                behind = [
                    jnp.where(lanes == 0, outside, turned[0]),
                    jnp.where(lanes == 0, turned[0], turned[1]),
                ]
                for half in range(2):
                    x = s[half]
                    spread = (
                        (ff[half] - flux_f[half, at, :])
                        + (fr[half] - flux_r[half, pl.ds(c + 7, count), :])
                        + (fc[half] - behind[half])
                    )
                    flux_f[half, at, :] = ff[half]
                    new[g, half, at, :] = x + RELAX * (goal[goal_at, half, at, :] - x + SMOOTH * spread)
            return carry0

        lax.fori_loop(0, g_count, body, 0)

    main_sweep(s_a, s_b, 0, 0, 9)
    main_sweep(s_b, s_a, 1, 1, 7)
    main_sweep(s_a, s_b, 2, 2, 5)

    for c in later:
        c.wait()
    sums[...] = jnp.zeros_like(sums)

    def finish(c, carry):
        chunk = 16
        at = pl.ds(pl.multiple_of(c * chunk, chunk), chunk)
        in_at = pl.ds(pl.multiple_of(c * chunk + TOP, 8), chunk)
        parts = []
        for f in range(frames):
            for half in range(2):
                cols = slice(half * 128, (half + 1) * 128)
                s = s_b[HALO + f, half, in_at, :]
                shrunk = s - jnp.clip(s, -shrink_level, shrink_level)
                out[f, at, cols] = shrunk
                r = own_video[f, at, cols] + dual_scale * own_multiplier[f, at, cols] - shrunk
                residual[half * frames + f, at, :] = r
                parts.append(r)
        for r in range(rank):
            images = [own_basis[r, at, half * 128 : (half + 1) * 128] for half in range(2)]
            for f in range(frames):
                term = images[0] * parts[2 * f] + images[1] * parts[2 * f + 1]
                sums[f * rank + r] += term[0:8] + term[8:16]
        return carry

    done, parts = [], 3
    for n in range(parts):
        lax.fori_loop(n * rows // 16 // parts, (n + 1) * rows // 16 // parts, finish, 0)
        at = pl.ds(n * rows // parts, rows // parts)
        done.append(copy(out.at[:, at, :], shrunk_out.at[:, at, :]))
    lines = jnp.sum(sums[...], axis=1)
    total = lax.dot_general(
        jnp.ones((8, 128), jnp.float32),
        lines,
        (((1,), (1,)), ((), ())),
        precision=HIGHEST,
        preferred_element_type=jnp.float32,
    )
    cross = jnp.concatenate([total[0:1] + ridge_part * coeff[...], jnp.zeros((1, 64), jnp.float32)], axis=1)
    owned = rows // slot_count
    chunk_rows = owned * 8 + 1

    def pack(j, carry):
        for f in range(frames):
            for half in range(2):
                sent[pl.ds(j * chunk_rows + half * frames + f, owned, stride=8), :] = residual[
                    half * frames + f, pl.ds(j * owned, owned), :
                ]
        sent[pl.ds(j * chunk_rows + owned * 8, 1), :] = cross
        return carry

    group = slot_count // 4
    for n in range(4):
        lax.fori_loop(n * group, (n + 1) * group, pack, 0)
        at = pl.ds(n * group * chunk_rows, group * chunk_rows)
        done.append(copy(sent.at[at], sent_out.at[at]))
    for c in done:
        c.wait()


def gram_kernel(slot_count, basis, out, old, sums, window):
    rank, rows, _ = basis.shape
    sums[...] = jnp.zeros_like(sums)

    def body(c, carry):
        at = pl.ds(pl.multiple_of(c * 8, 8), 8)
        images = [[basis[r, at, half * 128 : (half + 1) * 128] for half in range(2)] for r in range(rank)]
        for r in range(rank):
            for q in range(r, rank):
                sums[r * rank + q] += images[r][0] * images[q][0] + images[r][1] * images[q][1]
        return carry

    lax.fori_loop(0, rows // 8, body, 0)
    owned = rows // slot_count
    start = pl.multiple_of(lax.axis_index("frame") * owned // 8 * 8, 8)
    shift = lax.axis_index("frame") * owned - start
    flat = old.reshape(old.shape[0] * 2 * rank, 128)
    for half in range(2):
        for r in range(rank):
            window[half * rank + r, 0:16] = basis[r, pl.ds(start, 16), half * 128 : (half + 1) * 128]
            flat[pl.ds(half * rank + r, owned, stride=2 * rank), :] = window[half * rank + r, pl.ds(shift, owned), :]
    ones = jnp.ones((128, 128), jnp.float32)
    for r in range(rank):
        lines = jnp.concatenate(
            [jnp.sum(sums[min(r, q) * rank + max(r, q)], axis=0, keepdims=True) for q in range(rank)], axis=0
        )
        totals = dot(lines, ones)
        picked = jnp.where(iota((rank, 128), 0) == iota((rank, 128), 1), totals, 0.0)
        out[r : r + 1, :] = jnp.sum(picked, axis=0, keepdims=True)


def vmem(count):
    return [pl.BlockSpec(memory_space=pltpu.VMEM)] * count


def smem():
    return pl.BlockSpec(memory_space=pltpu.SMEM)


def anywhere(count):
    return [pl.BlockSpec(memory_space=pltpu.HBM)] * count


def floats(*shape):
    return jax.ShapeDtypeStruct(shape, jnp.float32)


LARGE = pltpu.CompilerParams(vmem_limit_bytes=28 * 1024 * 1024)
SMALL = pltpu.CompilerParams(vmem_limit_bytes=20 * 1024 * 1024)


def in_hbm(*shape):
    return pltpu.HBM(shape, jnp.float32)


def local(video, multiplier, foreground, basis, coefficients):
    plain = (video, multiplier)
    video, multiplier, basis = (pltpu.with_memory_space_constraint(x, pltpu.HBM) for x in (video, multiplier, basis))
    frames, rows, cols = video.shape
    rank = basis.shape[0]
    frame_count = lax.axis_size("frame")
    row_count = lax.axis_size("row")
    col_count = lax.axis_size("col")
    blocks = row_count * col_count
    all_rows = rows + 2 * TOP
    to_next = [(i, i + 1) for i in range(frame_count - 1)]
    to_previous = [(b, a) for a, b in to_next]
    to_right = [(i, i + 1) for i in range(col_count - 1)]
    to_left = [(b, a) for a, b in to_right]

    edge = pl.pallas_call(
        edge_kernel,
        out_shape=floats(2, frames, 8, cols),
        in_specs=[smem()] + anywhere(4),
        out_specs=vmem(1)[0],
        scratch_shapes=[pltpu.VMEM((n, 8, cols), jnp.float32) for n in (frames, frames, rank, frames)]
        + [pltpu.SemaphoreType.DMA((4,))],
        name="edge",
    )(coefficients, video, multiplier, basis, foreground)
    edge = lax.ppermute(edge, "row", [(0, 1), (1, 0)])
    down, images = pl.pallas_call(
        first_side_kernel,
        out_shape=(pltpu.VMEM((HALO + 2, rows, cols), jnp.float32), pltpu.VMEM(basis.shape, jnp.float32)),
        in_specs=[smem()] + vmem(2) + anywhere(1) + vmem(1),
        out_specs=vmem(2),
        scratch_shapes=[pltpu.SemaphoreType.DMA((6,))],
        compiler_params=SMALL,
        name="first_side",
    )(coefficients, *plain, basis, foreground)
    up = pl.pallas_call(
        second_side_kernel,
        out_shape=pltpu.VMEM((HALO + 2, rows, cols), jnp.float32),
        in_specs=[smem()] + vmem(4),
        out_specs=vmem(1)[0],
        compiler_params=SMALL,
        name="second_side",
    )(coefficients, *plain, images, foreground)
    up, edge = lax.optimization_barrier((up, edge))
    before = lax.ppermute(up, "frame", to_next)
    after = lax.ppermute(down, "frame", to_previous)
    right, left = pl.pallas_call(
        strips_kernel,
        out_shape=(floats(all_rows, 128), floats(all_rows, 128)),
        in_specs=vmem(3),
        out_specs=vmem(2),
        compiler_params=SMALL,
        name="strips",
    )(up, down, edge)
    from_left = lax.ppermute(right, "col", to_right)
    from_right = lax.ppermute(left, "col", to_left)
    folded = all_rows // 2
    ring, ring_up, ring_down = pl.pallas_call(
        ring_kernel,
        out_shape=(floats(all_rows + 16 * frames * 2, 128), floats(folded + 80, 128), floats(folded + 80, 128)),
        in_specs=vmem(5),
        out_specs=vmem(3),
        compiler_params=SMALL,
        name="ring",
    )(right, left, from_left, from_right, edge)
    ring_before = lax.ppermute(ring_up, "frame", to_next)
    ring_after = lax.ppermute(ring_down, "frame", to_previous)

    pixel_ridge = ridge_share * rows * cols * blocks
    owned_rows = rows // frame_count
    main = (2 * HALO + frames, 2, all_rows + 8, 128)
    strip = (all_rows + 8, 128)
    scratch = [
        main,
        main,
        (2 * HALO + frames - 2, 2, all_rows, 128),
        strip,
        strip,
        (all_rows, 128),
        (3, all_rows, 128),
        (2, all_rows, 128),
        (2, all_rows + 8, 128),
        video.shape,
        video.shape,
        basis.shape,
        (2 * frames, rows + 16, 128),
        video.shape,
        (frame_count * (owned_rows * 8 + 1) + 64, 128),
        (frames * rank, 8, 128),
    ]
    shrunk, sent = pl.pallas_call(
        functools.partial(sweep_kernel, pixel_ridge / blocks, frame_count, col_count),
        out_shape=(in_hbm(frames, rows, cols), in_hbm(frame_count * (owned_rows * 8 + 1), 128)),
        in_specs=anywhere(5) + vmem(3) + anywhere(3) + vmem(1),
        out_specs=anywhere(2),
        scratch_shapes=[pltpu.VMEM(s, jnp.float32) for s in scratch] + [pltpu.SemaphoreType.DMA((24,))],
        compiler_params=LARGE,
        name="sweeps",
    )(
        foreground,
        before,
        after,
        up,
        down,
        ring,
        ring_before,
        ring_after,
        video,
        multiplier,
        basis,
        coefficients.reshape(1, frames * rank),
    )
    got = lax.all_to_all(sent.reshape(frame_count, owned_rows * 8 + 1, 1, 128), "frame", 0, 0, tiled=True)
    basis, _ = lax.optimization_barrier((basis, sent))
    gram, old_owned = pl.pallas_call(
        functools.partial(gram_kernel, frame_count),
        out_shape=(floats(rank, 128), floats(16, 2 * rank, 128)),
        in_specs=vmem(1),
        out_specs=vmem(2),
        scratch_shapes=[
            pltpu.VMEM((rank * rank, 8, 128), jnp.float32),
            pltpu.VMEM((2 * rank, 24, 128), jnp.float32),
        ],
        compiler_params=SMALL,
        name="gram",
    )(basis)
    parts = jnp.concatenate([got[:, owned_rows * 8, 0, :], gram], axis=0)
    parts = lax.all_to_all(jnp.broadcast_to(parts[None], (blocks, *parts.shape)), ("row", "col"), 0, 0, tiled=True)
    frame_ridge = ridge_share * frames * frame_count
    new_basis, new_coeff = pl.pallas_call(
        functools.partial(final_kernel, pixel_ridge, frame_ridge),
        out_shape=(floats(owned_rows, rank, cols), floats(frames, rank)),
        in_specs=vmem(3),
        out_specs=vmem(2),
        scratch_shapes=[pltpu.VMEM((frame_count + 8, 128), jnp.float32)],
        compiler_params=SMALL,
        name="final",
    )(got.reshape(-1, 128), parts, old_owned)
    return shrunk, new_coeff, new_basis.transpose(1, 0, 2)


def solution(mesh):
    placed = (
        P("frame", "row", "col"),
        P("frame", "row", "col"),
        P("frame", "row", "col"),
        P(None, "row", "col"),
        P("frame", None),
    )
    return jax.shard_map(
        local,
        mesh=mesh,
        in_specs=placed,
        out_specs=(P("frame", "row", "col"), P("frame", None), P(None, ("row", "frame"), "col")),
        check_vma=False,
    )
```
